256 devices in a mesh: sector: 32 (over y, x, core), row: 8 (over z).
Axes of the slice: x: 4, y: 4, z: 8, core: 2. Of those that a mesh axis runs over, the one named last changes fastest.
Arguments:
- environment: bfloat16 [64, 4, 2048, 2048], P('sector', None, None, 'row')
- site_block: bfloat16 [64, 2048, 512], P('sector', 'row'), may hold values from -6 to 6
- next_site: bfloat16 [64, 512, 4096], P('sector', None, 'row'), may hold values from -6 to 6
- charges: int32 [64], replicated, may hold values from -32 to 31, as said below
- sizes: int32 [64], replicated, may hold values from 1024 to 2048, as said below
- pairs: int32 [64, 4], replicated, may hold values from 0 to 63, as said below
- owner: int32 [64], replicated, may hold values from 0 to 63, as said below
Outputs:
- isometry: float32 [2048, 64, 512], P('row', 'sector')
- advanced: bfloat16 [64, 512, 4096], P('sector', None, 'row')
The draws below stay inside these ranges and needn't reach their ends.
Inputs may be any that keep to these rules, and one draw needn't show every extreme that they name: `owner`: a permutation: every stored block index holds exactly one sector. All charges are distinct. `sizes`: multiples of 128; some sector has exactly 2048 rows and some has exactly 1024. `pairs`: row c lists the sectors whose charges differ from sector c's by -2, -1, 1 and 2, counted cyclically over the 64 charges.
All inputs are finite; a program needn't handle non-finite values.
Results may differ from the reference program's by a relative error of at most 0.0044.
Values may be sent and summed in bfloat16 or wider, within the bound.
A program may use at most 128 MiB of HBM per device.

```python
import jax
import jax.numpy as jnp
from jax import lax

W = 512
CAP = 2048
K = 4
NSEC = 64
NCOL = 4096


def sector_tables(key):
    key_owner = jax.random.fold_in(key, 101)
    key_charge = jax.random.fold_in(key, 202)
    key_units = jax.random.fold_in(key, 303)
    key_high = jax.random.fold_in(key, 404)
    key_low = jax.random.fold_in(key, 505)
    owner = jax.random.permutation(key_owner, NSEC).astype(jnp.int32)
    sector_of_charge = jax.random.permutation(key_charge, NSEC).astype(jnp.int32)
    shifted = jnp.argsort(sector_of_charge).astype(jnp.int32)
    charges = (shifted - NSEC // 2).astype(jnp.int32)
    deltas = jnp.array([-2, -1, 1, 2], dtype=jnp.int32)
    neighbour = (shifted[:, None] + deltas[None, :]) % NSEC
    pairs = sector_of_charge[neighbour].astype(jnp.int32)
    low_units = (max(CAP // 2, 2 * W) + 127) // 128
    high_units = CAP // 128
    units = jax.random.randint(key_units, (NSEC,), low_units, high_units + 1).astype(jnp.int32)
    high_pos = jax.random.randint(key_high, (), 0, NSEC).astype(jnp.int32)
    low_pos = (high_pos + 1 + jax.random.randint(key_low, (), 0, NSEC - 1).astype(jnp.int32)) % NSEC
    positions = jnp.arange(NSEC, dtype=jnp.int32)
    units = jnp.where(positions == high_pos, high_units, units)
    units = jnp.where(positions == low_pos, low_units, units)
    sizes = (units * 128).astype(jnp.int32)
    return (owner, charges, sizes, pairs)


def draw_owner(key, part):
    return sector_tables(key)[0]


def draw_charges(key, part):
    return sector_tables(key)[1]


def draw_sizes(key, part):
    return sector_tables(key)[2]


def draw_pairs(key, part):
    return sector_tables(key)[3]


def draw_environment(key, part):
    key_noise = jax.random.fold_in(key, 606)
    shape = (NSEC, K, CAP, CAP)
    noise = jax.random.normal(key_noise, shape, jnp.float32)
    values = jnp.eye(CAP, dtype=jnp.float32) + 0.4 * noise / jnp.sqrt(jnp.float32(CAP))
    return values.astype(jnp.bfloat16)


def levels(key, shape, cuts, least, largest):
    loudness, own = 1.0, jax.random.fold_in(key, 6)
    for axis_at, parts in cuts:
        draws = jnp.exp(jax.random.uniform(jax.random.fold_in(own, axis_at), (parts,), jnp.float32, least / len(cuts), largest / len(cuts)))
        loudness = loudness * jnp.repeat(draws, shape[axis_at] // parts).reshape([-1 if axis == axis_at else 1 for axis in range(len(shape))])
    return loudness


def centred(key, shape, scale, reach, split=(), held_as=jnp.bfloat16):
    drawn = jax.random.normal(key, shape, jnp.float32) * scale
    if len(split) > 0:
        drawn = levels(key, shape, split, -0.22, 0.18) * drawn
    return jnp.clip(drawn, min=-reach, max=reach).astype(held_as)


def setup_inputs(seed: int = 0) -> dict:
    keys = jax.random.split(jax.random.key(seed), 8)
    environment = draw_environment(jax.random.fold_in(keys[7], 71), 0)
    site_block = centred(keys[1], (NSEC, CAP, W), 1.0, 6.0, ((0, 32), (1, 8)))
    next_site = centred(keys[2], (NSEC, W, NCOL), 1.0, 6.0, ((0, 32), (2, 8)))
    charges = draw_charges(jax.random.fold_in(keys[7], 71), 0)
    sizes = draw_sizes(jax.random.fold_in(keys[7], 71), 0)
    pairs = draw_pairs(jax.random.fold_in(keys[7], 71), 0)
    owner = draw_owner(jax.random.fold_in(keys[7], 71), 0)
    return dict(environment=environment, site_block=site_block, next_site=next_site, charges=charges, sizes=sizes, pairs=pairs, owner=owner)


def reference(environment, site_block, next_site, charges, sizes, pairs, owner):
    sector_ids = jnp.arange(NSEC, dtype=jnp.int32)
    slot_ids = jnp.arange(NSEC, dtype=jnp.int32)
    slot_sector = lax.optimization_barrier(jnp.sum(jnp.where(owner[None, :] == slot_ids[:, None], sector_ids[None, :], 0), axis=1)).astype(jnp.int32)
    slot_size = sizes[slot_sector]
    row_ids = jnp.arange(CAP, dtype=jnp.int32)
    keep_rows = row_ids[None, :] < slot_size[:, None]
    masked_site = jnp.where(keep_rows[:, :, None], site_block, jnp.zeros((), site_block.dtype))

    def per_slot(slot):
        sector = slot_sector[slot]
        sources = pairs[sector]
        source_slots = owner[sources].astype(jnp.int32)
        picked = masked_site[source_slots].astype(jnp.float32)
        bond = jnp.einsum('kcr,krw->cw', environment[slot].astype(jnp.float32), picked, precision=lax.Precision.HIGHEST)
        chem_field = 2.0 * charges[sector].astype(jnp.float32) / NSEC
        bond = bond + chem_field * masked_site[slot].astype(jnp.float32)
        size_here = slot_size[slot]
        bond = jnp.where((row_ids < size_here)[:, None], bond, jnp.zeros((), jnp.float32))
        gram_matrix = jnp.dot(bond.T.astype(jnp.float32), bond.astype(jnp.float32), precision=lax.Precision.HIGHEST, preferred_element_type=jnp.float32)
        factor = jnp.linalg.cholesky(gram_matrix)
        ortho = lax.linalg.triangular_solve(factor, bond, left_side=False, lower=True, transpose_a=True)
        ortho = ortho * jnp.sqrt(size_here.astype(jnp.float32))
        trace_sum = jnp.trace(gram_matrix)
        scaling = lax.rsqrt(trace_sum / W + 1e-06)
        upper_bf = (factor.T * scaling).astype(jnp.bfloat16)
        moved = jnp.dot(upper_bf.astype(jnp.float32), next_site[slot].astype(jnp.float32), preferred_element_type=jnp.float32).astype(jnp.bfloat16)
        return (ortho, moved)
    ortho_all, advanced = lax.map(per_slot, slot_ids)
    isometry = jnp.transpose(ortho_all, (1, 0, 2))
    return (isometry, advanced)
```

```python
import jax
import jax.numpy as jnp
from jax import lax
from jax.experimental import pallas as pl
from jax.experimental.pallas import tpu as pltpu
from jax.sharding import PartitionSpec as P

NB = 4
T = 128
GROUP = 4
HI = lax.Precision.HIGHEST
PAIRS = [(p, i) for p in range(NB) for i in range(p, NB)]


def dot(a, b, dims, precision=HI):
    return lax.dot_general(
        a, b, (dims, ((), ())), precision=precision, preferred_element_type=jnp.float32
    )


def factor_tiles(a_tiles, u_ref, w_ref):
    count = len(a_tiles)
    rows8 = T // 8
    lane = lax.broadcasted_iota(jnp.int32, (8, T), 1)
    sub = lax.broadcasted_iota(jnp.int32, (8, T), 0)
    w_tiles = [
        [jnp.where(lane == sub + 8 * i, 1.0, 0.0).astype(jnp.float32) for i in range(rows8)]
        for _ in range(count)
    ]

    def spread(x, s):
        return jnp.broadcast_to(x[s : s + 1, :], (8, T))

    for j0 in range(0, T, GROUP):
        g = j0 // 8
        s0 = j0 - 8 * g
        state = []
        for m in range(count):
            cols = [
                [
                    jnp.broadcast_to(a_tiles[m][i][:, j0 + k : j0 + k + 1], (8, T))
                    for i in range(g, rows8)
                ]
                for k in range(GROUP)
            ]
            rows = [spread(a_tiles[m][g], s0 + k) for k in range(GROUP)]
            wrows = [spread(w_tiles[m][g], s0 + k) for k in range(GROUP)]
            state.append((cols, rows, wrows))
        for k in range(GROUP):
            for m in range(count):
                cols, rows, wrows = state[m]
                rs = lax.rsqrt(spread(cols[k][0], s0 + k))
                cols[k] = [c * rs for c in cols[k]]
                rows[k] = rows[k] * rs
                wrows[k] = wrows[k] * rs
                for q in range(k + 1, GROUP):
                    f = spread(cols[k][0], s0 + q)
                    cols[q] = [c - l * f for c, l in zip(cols[q], cols[k])]
                    rows[q] = rows[q] - rows[k] * f
                    wrows[q] = wrows[q] - wrows[k] * f
        for m in range(count):
            cols, rows, wrows = state[m]
            for k in range(GROUP):
                j = j0 + k
                keep = lane[:1] >= j
                u_ref[m, j : j + 1, :] = jnp.where(keep, rows[k][:1], 0.0)
                w_ref[m, j : j + 1, :] = wrows[k][:1]
            last = s0 + GROUP == 8
            for i in range(g + 1 if last else g, rows8):
                a, w = a_tiles[m][i], w_tiles[m][i]
                for k in range(GROUP):
                    l = cols[k][i - g]
                    if i == g:
                        l = jnp.where(sub >= s0 + GROUP, l, 0.0)
                    a = a - l * rows[k]
                    w = w - l * wrows[k]
                a_tiles[m][i], w_tiles[m][i] = a, w


def tail_kernel(g_ref, b_ref, next_ref, root_ref, iso_ref, adv_ref, s_ref, d_ref, u_ref, w_ref):
    count = g_ref.shape[0]
    eye = lax.broadcasted_iota(jnp.int32, (T, T), 0) == lax.broadcasted_iota(jnp.int32, (T, T), 1)
    scales = []
    for m in range(count):
        trace = jnp.zeros((), jnp.float32)
        for n, (p, i) in enumerate(PAIRS):
            s_ref[m, p, i] = g_ref[m, n]
            if p == i:
                trace = trace + jnp.sum(jnp.where(eye, g_ref[m, n], 0.0))
        scales.append(lax.rsqrt(jnp.full((1, T), trace / (NB * T) + 1e-6, jnp.float32)))

    def block(p, carry):
        tiles = [[s_ref[m, p, p, 8 * i : 8 * i + 8, :] for i in range(T // 8)] for m in range(count)]
        factor_tiles(tiles, u_ref, w_ref)
        for m in range(count):
            d_ref[m, p] = w_ref[m]
            s_ref[m, p, p] = u_ref[m]

        def panel(i, c):
            for m in range(count):
                s_ref[m, p, i] = dot(w_ref[m], s_ref[m, p, i], ((1,), (0,)))
            return c

        lax.fori_loop(p + 1, NB, panel, 0)

        def trail(i, c):
            def inner(k, c2):
                for m in range(count):
                    s_ref[m, i, k] = s_ref[m, i, k] - dot(s_ref[m, p, i], s_ref[m, p, k], ((0,), (0,)))
                return c2

            return lax.fori_loop(i, NB, inner, c)

        lax.fori_loop(p + 1, NB, trail, 0)
        return carry

    lax.fori_loop(0, NB, block, 0)
    for m in range(count):
        solved = []
        for j in range(NB):
            x = b_ref[m, :, T * j : T * j + T]
            for i in range(j):
                x = x - dot(solved[i], s_ref[m, i, j], ((1,), (0,)))
            x = dot(x, d_ref[m, j], ((1,), (1,)))
            solved.append(x)
            iso_ref[m, :, T * j : T * j + T] = x * root_ref[m]
        for p in range(NB):
            total = None
            for i in range(p, NB):
                up = (s_ref[m, p, i] * scales[m]).astype(jnp.bfloat16)
                term = dot(up, next_ref[m, T * i : T * i + T, :], ((1,), (0,)), None)
                total = term if total is None else total + term
            adv_ref[m, T * p : T * p + T, :] = total.astype(jnp.bfloat16)


def tail(gram, bond, next_site, root):
    count, rows, window = bond.shape
    vmem = pl.BlockSpec(memory_space=pltpu.VMEM)
    return pl.pallas_call(
        tail_kernel,
        out_shape=(
            jax.ShapeDtypeStruct((count, rows, window), jnp.float32),
            jax.ShapeDtypeStruct(next_site.shape, jnp.bfloat16),
        ),
        in_specs=[vmem] * 4,
        out_specs=(vmem, vmem),
        scratch_shapes=[
            pltpu.VMEM((count, NB, NB, T, T), jnp.float32),
            pltpu.VMEM((count, NB, T, T), jnp.float32),
            pltpu.VMEM((count, T, T), jnp.float32),
            pltpu.VMEM((count, T, T), jnp.float32),
        ],
        compiler_params=pltpu.CompilerParams(vmem_limit_bytes=40 * 1024 * 1024),
        name="tail",
    )(gram, bond, next_site, root)


def lookup(values_table, indices):
    positions = jnp.arange(values_table.shape[0], dtype=jnp.int32)
    return jnp.sum(jnp.where(indices[..., None] == positions, values_table, 0), axis=-1)


def local(environment, site_block, next_site, charges, sizes, pairs, owner):
    per_group, rows_local, window = site_block.shape
    sector_count = per_group * lax.axis_size("sector")
    group_index = lax.axis_index("sector")
    row_index = lax.axis_index("row")
    sector_ids = jnp.arange(sector_count, dtype=jnp.int32)
    my_slots = group_index * per_group + jnp.arange(per_group, dtype=jnp.int32)
    my_sectors = jnp.sum(
        jnp.where(owner[None, :] == my_slots[:, None], sector_ids[None, :], 0), axis=1
    )
    target_size = lookup(sizes, my_sectors)
    chosen = (my_sectors[:, None] == sector_ids[None, :])[:, :, None]
    source_sectors = jnp.sum(jnp.where(chosen, pairs[None, :, :], 0), axis=1)
    source_slots = lookup(owner, source_sectors)
    chem_field = 2.0 * lookup(charges, my_sectors).astype(jnp.float32) / sector_count
    root = jnp.sqrt(target_size.astype(jnp.float32))
    local_rows = row_index * rows_local + jnp.arange(rows_local, dtype=jnp.int32)
    keep_rows = (local_rows[None, :] < target_size[:, None])[:, :, None]
    site_kept = jnp.where(keep_rows, site_block, jnp.zeros((), site_block.dtype))
    gathered = lax.all_gather(site_kept, "sector", axis=0, tiled=True)
    picked = jnp.take(gathered, source_slots, axis=0)
    partial_sum = jnp.einsum(
        "ikcr,ikrw->icw", environment, picked, preferred_element_type=jnp.float32
    ).astype(jnp.bfloat16)
    summed = lax.psum_scatter(partial_sum, "row", scatter_dimension=1, tiled=True)
    bond = summed.astype(jnp.float32) + chem_field[:, None, None] * site_kept.astype(jnp.float32)
    bond = jnp.where(keep_rows, bond, 0.0)
    part = jnp.einsum("iws,iwt->ist", bond, bond, precision=HI)
    packed = jnp.stack(
        [part[:, T * p : T * p + T, T * i : T * i + T] for p, i in PAIRS], axis=1
    )
    packed = lax.psum(packed, "row")
    wide_root = jnp.broadcast_to(root[:, None, None], (per_group, 1, T))
    iso, advanced = tail(packed, bond, next_site, wide_root)
    return (jnp.swapaxes(iso, 0, 1), advanced)


def solution(mesh):
    return jax.shard_map(
        local,
        mesh=mesh,
        in_specs=(
            P("sector", None, None, "row"),
            P("sector", "row", None),
            P("sector", None, "row"),
            P(),
            P(),
            P(),
            P(),
        ),
        out_specs=(P("row", "sector", None), P("sector", None, "row")),
        check_vma=False,
    )
```

```python
import jax
import jax.numpy as jnp
from jax import lax
from jax.experimental import pallas as pl
from jax.experimental.pallas import tpu as pltpu
from jax.sharding import PartitionSpec as P

NB = 4
T = 128
GROUP = 4
HI = lax.Precision.HIGHEST
PAIRS = [(p, i) for p in range(NB) for i in range(p, NB)]


def dot(a, b, dims, precision=HI):
    return lax.dot_general(
        a, b, (dims, ((), ())), precision=precision, preferred_element_type=jnp.float32
    )


def factor_tiles(a_tiles, u_ref, w_ref):
    count = len(a_tiles)
    rows8 = T // 8
    lane = lax.broadcasted_iota(jnp.int32, (8, T), 1)
    sub = lax.broadcasted_iota(jnp.int32, (8, T), 0)
    w_tiles = [
        [jnp.where(lane == sub + 8 * i, 1.0, 0.0).astype(jnp.float32) for i in range(rows8)]
        for _ in range(count)
    ]

    def spread(x, s):
        return jnp.broadcast_to(x[s : s + 1, :], (8, T))

    for j0 in range(0, T, GROUP):
        g = j0 // 8
        s0 = j0 - 8 * g
        state = []
        for m in range(count):
            cols = [
                [
                    jnp.broadcast_to(a_tiles[m][i][:, j0 + k : j0 + k + 1], (8, T))
                    for i in range(g, rows8)
                ]
                for k in range(GROUP)
            ]
            rows = [spread(a_tiles[m][g], s0 + k) for k in range(GROUP)]
            wrows = [spread(w_tiles[m][g], s0 + k) for k in range(GROUP)]
            state.append((cols, rows, wrows))
        for k in range(GROUP):
            for m in range(count):
                cols, rows, wrows = state[m]
                rs = lax.rsqrt(spread(cols[k][0], s0 + k))
                cols[k] = [c * rs for c in cols[k]]
                rows[k] = rows[k] * rs
                wrows[k] = wrows[k] * rs
                for q in range(k + 1, GROUP):
                    f = spread(cols[k][0], s0 + q)
                    cols[q] = [c - l * f for c, l in zip(cols[q], cols[k])]
                    rows[q] = rows[q] - rows[k] * f
                    wrows[q] = wrows[q] - wrows[k] * f
        for m in range(count):
            cols, rows, wrows = state[m]
            for k in range(GROUP):
                j = j0 + k
                keep = lane[:1] >= j
                u_ref[m, j : j + 1, :] = jnp.where(keep, rows[k][:1], 0.0)
                w_ref[m, j : j + 1, :] = wrows[k][:1]
            last = s0 + GROUP == 8
            for i in range(g + 1 if last else g, rows8):
                a, w = a_tiles[m][i], w_tiles[m][i]
                for k in range(GROUP):
                    l = cols[k][i - g]
                    if i == g:
                        l = jnp.where(sub >= s0 + GROUP, l, 0.0)
                    a = a - l * rows[k]
                    w = w - l * wrows[k]
                a_tiles[m][i], w_tiles[m][i] = a, w


def tail_kernel(g_ref, b_ref, next_ref, root_ref, iso_ref, adv_ref, s_ref, d_ref, u_ref, w_ref):
    count = b_ref.shape[0]
    eye = lax.broadcasted_iota(jnp.int32, (T, T), 0) == lax.broadcasted_iota(jnp.int32, (T, T), 1)
    scales = []
    for m in range(count):
        trace = jnp.zeros((), jnp.float32)
        for n, (p, i) in enumerate(PAIRS):
            for q in range(T // 16):
                s_ref[m, p, i, 16 * q : 16 * q + 16, :] = g_ref[q, m, n]
            if p == i:
                trace = trace + jnp.sum(jnp.where(eye, s_ref[m, p, i], 0.0))
        scales.append(lax.rsqrt(jnp.full((1, T), trace / (NB * T) + 1e-6, jnp.float32)))

    def block(p, carry):
        tiles = [[s_ref[m, p, p, 8 * i : 8 * i + 8, :] for i in range(T // 8)] for m in range(count)]
        factor_tiles(tiles, u_ref, w_ref)
        for m in range(count):
            d_ref[m, p] = w_ref[m]
            s_ref[m, p, p] = u_ref[m]

        def panel(i, c):
            for m in range(count):
                s_ref[m, p, i] = dot(w_ref[m], s_ref[m, p, i], ((1,), (0,)))
            return c

        lax.fori_loop(p + 1, NB, panel, 0)

        def trail(i, c):
            def inner(k, c2):
                for m in range(count):
                    s_ref[m, i, k] = s_ref[m, i, k] - dot(s_ref[m, p, i], s_ref[m, p, k], ((0,), (0,)))
                return c2

            return lax.fori_loop(i, NB, inner, c)

        lax.fori_loop(p + 1, NB, trail, 0)
        return carry

    lax.fori_loop(0, NB, block, 0)
    for m in range(count):
        solved = []
        for j in range(NB):
            x = b_ref[m, :, T * j : T * j + T]
            for i in range(j):
                x = x - dot(solved[i], s_ref[m, i, j], ((1,), (0,)))
            x = dot(x, d_ref[m, j], ((1,), (1,)))
            solved.append(x)
            iso_ref[m, :, T * j : T * j + T] = x * root_ref[m]
        for p in range(NB):
            total = None
            for i in range(p, NB):
                up = (s_ref[m, p, i] * scales[m]).astype(jnp.bfloat16)
                term = dot(up, next_ref[m, T * i : T * i + T, :], ((1,), (0,)), None)
                total = term if total is None else total + term
            adv_ref[m, T * p : T * p + T, :] = total.astype(jnp.bfloat16)


def tail(gram, bond, next_site, root):
    count, rows, window = bond.shape
    vmem = pl.BlockSpec(memory_space=pltpu.VMEM)
    return pl.pallas_call(
        tail_kernel,
        out_shape=(
            jax.ShapeDtypeStruct((count, rows, window), jnp.float32),
            jax.ShapeDtypeStruct(next_site.shape, jnp.bfloat16),
        ),
        in_specs=[vmem] * 4,
        out_specs=(vmem, vmem),
        scratch_shapes=[
            pltpu.VMEM((count, NB, NB, T, T), jnp.float32),
            pltpu.VMEM((count, NB, T, T), jnp.float32),
            pltpu.VMEM((count, T, T), jnp.float32),
            pltpu.VMEM((count, T, T), jnp.float32),
        ],
        compiler_params=pltpu.CompilerParams(vmem_limit_bytes=40 * 1024 * 1024),
        name="tail",
    )(gram, bond, next_site, root)


CHUNKS = 4
NZ = 8
SIDE = 4
ROWS = 256
MESH = pl.DeviceIdType.MESH
FLOWS = [(0, 0), (1, 1), (0, 1), (1, 0)]


def first_hop(direction, t):
    return 1 if direction == t else 2


def ordered(tasks):
    rate = {"x": 47.0, "y": 47.0, "z": 47.0, "c": 300.0}
    link_free, arrival, done, order = {}, {}, set(), []
    now, left = 0.0, list(tasks)
    while left:
        best = None
        for n, task in enumerate(left):
            if all(a in done for a in task["after"]) and all(k in arrival for k in task["needs"]):
                start = max([now] + [arrival[k] for k in task["needs"]])
                if best is None or start < best[0]:
                    best = (start, n)
        start, n = best
        task = left.pop(n)
        now = start + task["time"]
        for key, link, kib in task["sends"]:
            begin = max(now, link_free.get(link, 0.0))
            link_free[link] = begin + kib / rate[link[0]]
            arrival[key] = link_free[link] + (1.0 if link[0] == "c" else 1.8)
        done.add(task["name"])
        order.append(task)
    return order


def bond_kernel(
    src_ref, env_ref, site_ref, extra_ref, keep_ref, bond_ref, gram_ref,
    g0, g1, g2, g3, env_v, part, send_b, recv_b, gp, gsend, grecv, gfull,
    env_sem, own_sem, ag_send, ag_recv, rs_send, rs_recv, gr_send, gr_recv, gg_send, gg_recv,
):
    gath = (g0, g1, g2, g3)
    sector, z = lax.axis_index("sector"), lax.axis_index("row")
    c = sector % 2
    x = (sector // 2) % SIDE
    y = sector // (2 * SIDE)

    def at(xx, yy, cc):
        return {"sector": ((yy % SIDE) * SIDE + xx % SIDE) * 2 + cc}

    def along(m, dmaj, dmin):
        return at(x + dmin, y + dmaj, c) if m == 0 else at(x + dmaj, y + dmin, c)

    major, minor = (y, x), (x, y)
    partner = at(x, y, 1 - c)
    up, down = {"row": (z + 1) % NZ}, {"row": (z + NZ - 1) % NZ}

    def slot(m, maj, mino):
        return 32 * m + ((maj % SIDE) * 2 + c) * SIDE + mino % SIDE

    barrier = pltpu.get_barrier_semaphore()
    env_copy = pltpu.make_async_copy(env_ref, env_v, env_sem)
    env_copy.start()
    own = []
    for j in range(CHUNKS):
        for m in range(2):
            own.append(
                pltpu.make_async_copy(
                    site_ref.at[j, m], gath[j].at[slot(m, major[m], minor[m])], own_sem.at[j, m]
                )
            )
            own[-1].start()
    partners = [along(0, 0, 1), along(0, 0, 3), along(0, 1, 0), along(0, 3, 0), partner, up, down]
    for device in partners:
        pl.semaphore_signal(barrier, inc=1, device_id=device, device_id_type=MESH)
    pl.semaphore_wait(barrier, len(partners))

    copies = {}

    def send(key, src, dst, ssem, rsem, device):
        copy = pltpu.make_async_remote_copy(
            src_ref=src, dst_ref=dst, send_sem=ssem, recv_sem=rsem, device_id=device, device_id_type=MESH
        )
        copy.start()
        copies[key] = copy

    def ag_send_one(j, m, n, ref, device, src=None):
        send((j, m, n), ref if src is None else src, ref, ag_send.at[j, m, n], ag_recv.at[j, m, n], device)

    def a1(j):
        for m in range(2):
            ref = gath[j].at[slot(m, major[m], minor[m])]
            ag_send_one(j, m, 0, ref, along(m, 0, 1), site_ref.at[j, m])
            ag_send_one(j, m, 1, ref, along(m, 0, 3), site_ref.at[j, m])

    def a2(j):
        for m in range(2):
            copies[j, m, 0].wait_recv()
            low = gath[j].at[slot(m, major[m], minor[m] + 3), pl.ds(0, ROWS // 2)]
            ag_send_one(j, m, 2, low, along(m, 0, 1))
            copies[j, m, 1].wait_recv()
            high = gath[j].at[slot(m, major[m], minor[m] + 1), pl.ds(ROWS // 2, ROWS // 2)]
            ag_send_one(j, m, 3, high, along(m, 0, 3))

    def group(j, m, dmaj, start=0, size=SIDE):
        return gath[j].at[pl.ds(slot(m, major[m] + dmaj, 0) + start, size)]

    def b1(j):
        for m in range(2):
            own[2 * j + m].wait()
            copies[j, m, 2].wait_recv()
            copies[j, m, 3].wait_recv()
            ag_send_one(j, m, 4, group(j, m, 0), along(m, 1, 0))
            ag_send_one(j, m, 5, group(j, m, 0), along(m, 3, 0))
            ag_send_one(j, m, 8, group(j, m, 0), partner)

    def b2(j):
        for m in range(2):
            copies[j, m, 4].wait_recv()
            ag_send_one(j, m, 6, group(j, m, 3, 0, 2), along(m, 1, 0))
            copies[j, m, 5].wait_recv()
            ag_send_one(j, m, 7, group(j, m, 1, 2, 2), along(m, 3, 0))
            ag_send_one(j, m, 9, group(j, m, 3), partner)
            ag_send_one(j, m, 10, group(j, m, 1), partner)

    def b3(j):
        for m in range(2):
            copies[j, m, 6].wait_recv()
            copies[j, m, 7].wait_recv()
            ag_send_one(j, m, 11, group(j, m, 2), partner)

    def ready(j):
        for m in range(2):
            for n in (8, 9, 10, 11):
                copies[j, m, n].wait_recv()
        if j == 0:
            env_copy.wait()

    def multiply(j, r):
        def one(n, carry):
            t = n % 2
            o = (n // 2) * (NZ - 2 * r) + r
            first = pl.multiple_of(((z + o) % NZ) * ROWS, ROWS)
            total = None
            for k in range(4):
                term = jnp.dot(
                    env_v[t, k, pl.ds(first, ROWS), :],
                    gath[j][src_ref[t, k]],
                    preferred_element_type=jnp.float32,
                )
                total = term if total is None else total + term
            part[j, o, t] = total
            return carry

        lax.fori_loop(0, 2 if r in (0, 4) else 4, one, 0)

    def hop(j, s, direction, t):
        o = 5 - s if direction == 0 else 3 + s
        value = part[j, o, t]
        if s > first_hop(direction, t):
            copies["r", j, s - 1, direction, t].wait_recv()
            value = value + recv_b[j, direction, t, s - 2].astype(jnp.float32)
        send_b[j, direction, t, s - 1] = value.astype(jnp.bfloat16)
        send(
            ("r", j, s, direction, t),
            send_b.at[j, direction, t, s - 1],
            recv_b.at[j, direction, t, s - 1],
            rs_send.at[j, direction, t, s - 1],
            rs_recv.at[j, direction, t, s - 1],
            up if direction == 0 else down,
        )

    def finish(j, t):
        copies["r", j, 4, 0, t].wait_recv()
        copies["r", j, 4, 1, t].wait_recv()
        cols = pl.ds(T * j, T)
        total = part[j, 0, t] + extra_ref[t, :, cols]
        total = total + recv_b[j, 0, t, 3].astype(jnp.float32) + recv_b[j, 1, t, 3].astype(jnp.float32)
        bond_ref[t, :, cols] = jnp.where(keep_ref[t] > 0.5, total, 0.0)

    def grams(j):
        for t in range(2):
            for i in range(j + 1):
                value = dot(bond_ref[t, :, T * i : T * i + T], bond_ref[t, :, T * j : T * j + T], ((0,), (0,)))
                n = PAIRS.index((i, j))
                for q in range(NZ):
                    gp[q, t, n] = value[16 * q : 16 * q + 16]

    tasks = []

    def task(name, emit, time, needs=(), after=(), sends=()):
        tasks.append(dict(name=name, emit=emit, time=time, needs=needs, after=after, sends=sends))

    def axes(m):
        return ("x", "y") if m == 0 else ("y", "x")

    for j in range(CHUNKS):
        ms = range(2)
        mins, majs = [axes(m)[0] for m in ms], [axes(m)[1] for m in ms]
        task(("a1", j), lambda j=j: a1(j), 0.1, after=[("b1", j - 1)] if j else [],
             sends=[((j, m, n), mins[m] + str(n), 64) for m in ms for n in (0, 1)])
        task(("a2", j), lambda j=j: a2(j), 0.1, needs=[(j, m, n) for m in ms for n in (0, 1)],
             sends=[((j, m, n + 2), mins[m] + str(n), 32) for m in ms for n in (0, 1)])
        task(("b1", j), lambda j=j: b1(j), 0.1, needs=[(j, m, n) for m in ms for n in (2, 3)],
             after=[("b2", j - 1)] if j else [],
             sends=[((j, m, n + 4), majs[m] + str(n), 256) for m in ms for n in (0, 1)]
             + [((j, m, 8), "c", 256) for m in ms])
        task(("b2", j), lambda j=j: b2(j), 0.1, needs=[(j, m, n) for m in ms for n in (4, 5)],
             sends=[((j, m, n + 6), majs[m] + str(n), 128) for m in ms for n in (0, 1)]
             + [((j, m, n), "c", 256) for m in ms for n in (9, 10)])
        task(("b3", j), lambda j=j: b3(j), 0.1, needs=[(j, m, n) for m in ms for n in (6, 7)],
             sends=[((j, m, 11), "c", 256) for m in ms])
        task(("ready", j), lambda j=j: ready(j), 0.1, needs=[(j, m, n) for m in ms for n in (8, 9, 10, 11)])
        before = ("ready", j)
        for r in (4, 3, 2, 1, 0):
            task(("mm", j, r), lambda j=j, r=r: multiply(j, r), 0.4 if r in (0, 4) else 0.8, after=[before])
            before = ("mm", j, r)
            if r == 0:
                continue
            s = 5 - r
            for direction, t in FLOWS:
                if s >= first_hop(direction, t):
                    more = s > first_hop(direction, t)
                    task(("hop", j, s, direction, t),
                         lambda j=j, s=s, direction=direction, t=t: hop(j, s, direction, t), 0.1,
                         needs=[("r", j, s - 1, direction, t)] if more else [], after=[before],
                         sends=[(("r", j, s, direction, t), "z" + str(direction), 64)])
        for t in range(2):
            task(("finish", j, t), lambda j=j, t=t: finish(j, t), 0.1,
                 needs=[("r", j, 4, 0, t), ("r", j, 4, 1, t)], after=[("mm", j, 0)])
        task(("gram", j), lambda j=j: grams(j), 0.4 + 0.4 * j,
             after=[("finish", j, 0), ("finish", j, 1)] + ([("gram", j - 1)] if j else []))
    for item in ordered(tasks):
        item["emit"]()

    for s in range(1, 5):
        for direction, t in FLOWS:
            if s < first_hop(direction, t):
                continue
            o = 5 - s if direction == 0 else 3 + s
            value = gp[(z + o) % NZ, t]
            if s > first_hop(direction, t):
                copies["g", s - 1, direction, t].wait_recv()
                value = value + grecv[direction, t, s - 2]
            gsend[direction, t, s - 1] = value
            send(
                ("g", s, direction, t), gsend.at[direction, t, s - 1], grecv.at[direction, t, s - 1],
                gr_send.at[direction, t, s - 1], gr_recv.at[direction, t, s - 1],
                up if direction == 0 else down,
            )
    for t in range(2):
        copies["g", 4, 0, t].wait_recv()
        copies["g", 4, 1, t].wait_recv()
        gfull[z, t] = gp[z, t] + grecv[0, t, 3] + grecv[1, t, 3]
    for s in range(1, 5):
        for direction, t in FLOWS:
            if s == 4 and direction != t:
                continue
            if s > 1:
                copies["f", s - 1, direction, t].wait_recv()
            q = (z + NZ - (s - 1)) % NZ if direction == 0 else (z + s - 1) % NZ
            send(
                ("f", s, direction, t), gfull.at[q, t], gfull.at[q, t],
                gg_send.at[direction, t, s - 1], gg_recv.at[direction, t, s - 1],
                up if direction == 0 else down,
            )
    for direction, t in FLOWS:
        copies["f", 4 if direction == t else 3, direction, t].wait_recv()
    for copy in copies.values():
        copy.wait_send()
    gram_ref[...] = gfull[...]


def bond_and_gram(sources, environment, sites, extra, keep):
    per_group, _, capacity, rows = environment.shape
    vmem, anywhere = pl.BlockSpec(memory_space=pltpu.VMEM), pl.BlockSpec(memory_space=pl.ANY)
    bf, f32 = jnp.bfloat16, jnp.float32
    dma = pltpu.SemaphoreType.DMA
    blocks = len(PAIRS)
    return pl.pallas_call(
        bond_kernel,
        out_shape=(
            jax.ShapeDtypeStruct(extra.shape, f32),
            jax.ShapeDtypeStruct((NZ, 2, blocks, 16, T), f32),
        ),
        in_specs=[pl.BlockSpec(memory_space=pltpu.SMEM), anywhere, vmem, vmem, vmem],
        out_specs=(vmem, vmem),
        scratch_shapes=[pltpu.VMEM((64, ROWS, T), bf)] * CHUNKS
        + [
            pltpu.VMEM(environment.shape, bf),
            pltpu.VMEM((CHUNKS, NZ, 2, ROWS, T), f32),
            pltpu.VMEM((CHUNKS, 2, 2, 4, ROWS, T), bf),
            pltpu.VMEM((CHUNKS, 2, 2, 4, ROWS, T), bf),
            pltpu.VMEM((NZ, 2, blocks, 16, T), f32),
            pltpu.VMEM((2, 2, 4, blocks, 16, T), f32),
            pltpu.VMEM((2, 2, 4, blocks, 16, T), f32),
            pltpu.VMEM((NZ, 2, blocks, 16, T), f32),
            dma,
            dma((CHUNKS, 2)),
            dma((CHUNKS, 2, 12)),
            dma((CHUNKS, 2, 12)),
            dma((CHUNKS, 2, 2, 4)),
            dma((CHUNKS, 2, 2, 4)),
            dma((2, 2, 4)),
            dma((2, 2, 4)),
            dma((2, 2, 4)),
            dma((2, 2, 4)),
        ],
        compiler_params=pltpu.CompilerParams(
            vmem_limit_bytes=62 * 1024 * 1024, collective_id=0, has_side_effects=True
        ),
        name="bond",
    )(sources, environment, sites, extra, keep)


def lookup(values_table, indices):
    positions = jnp.arange(values_table.shape[0], dtype=jnp.int32)
    return jnp.sum(jnp.where(indices[..., None] == positions, values_table, 0), axis=-1)


def local(environment, site_block, next_site, charges, sizes, pairs, owner):
    per_group, rows_local, window = site_block.shape
    sector_count = per_group * lax.axis_size("sector")
    group_index = lax.axis_index("sector")
    row_index = lax.axis_index("row")
    sector_ids = jnp.arange(sector_count, dtype=jnp.int32)
    my_slots = group_index * per_group + jnp.arange(per_group, dtype=jnp.int32)
    my_sectors = jnp.sum(
        jnp.where(owner[None, :] == my_slots[:, None], sector_ids[None, :], 0), axis=1
    )
    target_size = lookup(sizes, my_sectors)
    chosen = (my_sectors[:, None] == sector_ids[None, :])[:, :, None]
    source_sectors = jnp.sum(jnp.where(chosen, pairs[None, :, :], 0), axis=1)
    source_slots = lookup(owner, source_sectors)
    chem_field = 2.0 * lookup(charges, my_sectors).astype(jnp.float32) / sector_count
    root = jnp.sqrt(target_size.astype(jnp.float32))
    local_rows = row_index * rows_local + jnp.arange(rows_local, dtype=jnp.int32)
    keep_rows = (local_rows[None, :] < target_size[:, None])[:, :, None]
    site_kept = jnp.where(keep_rows, site_block, jnp.zeros((), site_block.dtype))
    slots = source_slots
    m, core = slots % 2, (slots // 2) % 2
    x, y = (slots // 4) % SIDE, slots // (4 * SIDE)
    sources = jnp.where(m == 0, (y * 2 + core) * SIDE + x, 32 + (x * 2 + core) * SIDE + y)
    sites = jnp.transpose(site_kept.reshape(per_group, rows_local, CHUNKS, T), (2, 0, 1, 3))
    extra = chem_field[:, None, None] * site_kept.astype(jnp.float32)
    keep = jnp.broadcast_to(keep_rows.astype(jnp.float32), (per_group, rows_local, T))
    bond, gram = bond_and_gram(sources, environment, sites, extra, keep)
    wide_root = jnp.broadcast_to(root[:, None, None], (per_group, 1, T))
    iso, advanced = tail(gram, bond, next_site, wide_root)
    return (jnp.swapaxes(iso, 0, 1), advanced)


def solution(mesh):
    return jax.shard_map(
        local,
        mesh=mesh,
        in_specs=(
            P("sector", None, None, "row"),
            P("sector", "row", None),
            P("sector", None, "row"),
            P(),
            P(),
            P(),
            P(),
        ),
        out_specs=(P("row", "sector", None), P("sector", None, "row")),
        check_vma=False,
    )
```

```python
import jax
import jax.numpy as jnp
from jax import lax
from jax.experimental import pallas as pl
from jax.experimental.pallas import tpu as pltpu
from jax.sharding import PartitionSpec as P

NB = 4
T = 128
GROUP = 8
HALF = 64
HI = lax.Precision.HIGHEST
PAIRS = [(p, i) for i in range(NB) for p in range(i + 1)]


def dot(a, b, dims, precision=HI):
    return lax.dot_general(
        a, b, (dims, ((), ())), precision=precision, preferred_element_type=jnp.float32
    )


def factor_tiles(a_tiles, r_ref):
    count = len(a_tiles)
    rows8 = HALF // 8
    lane = lax.broadcasted_iota(jnp.int32, (8, T), 1)
    sub = lax.broadcasted_iota(jnp.int32, (8, T), 0)

    def spread(x, s):
        return jnp.broadcast_to(x[s : s + 1, :], (8, T))

    for j0 in range(0, HALF, GROUP):
        g = j0 // 8
        s0 = j0 - 8 * g
        state = []
        for m in range(count):
            cols = [
                [
                    jnp.broadcast_to(a_tiles[m][i][:, j0 + k : j0 + k + 1], (8, T))
                    for i in range(g, rows8)
                ]
                for k in range(GROUP)
            ]
            rows = [spread(a_tiles[m][g], s0 + k) for k in range(GROUP)]
            state.append((cols, rows))
        for k in range(GROUP):
            for m in range(count):
                cols, rows = state[m]
                rs = lax.rsqrt(spread(cols[k][0], s0 + k))
                cols[k] = [c * rs for c in cols[k]]
                rows[k] = rows[k] * rs
                for q in range(k + 1, GROUP):
                    f = spread(cols[k][0], s0 + q)
                    cols[q] = [c - l * f for c, l in zip(cols[q], cols[k])]
                    rows[q] = rows[q] - rows[k] * f
        for m in range(count):
            cols, rows = state[m]
            for k in range(GROUP):
                j = j0 + k
                r_ref[m, j : j + 1, :] = jnp.where(lane[:1] >= j, rows[k][:1], 0.0)
            last = s0 + GROUP == 8
            for i in range(g + 1 if last else g, rows8):
                a = a_tiles[m][i]
                for k in range(GROUP):
                    l = cols[k][i - g]
                    if i == g:
                        l = jnp.where(sub >= s0 + GROUP, l, 0.0)
                    a = a - l * rows[k]
                a_tiles[m][i] = a


def factor_block(a_list, u_ref, w_ref, r_ref):
    lane = lax.broadcasted_iota(jnp.int32, (HALF, T), 1)
    row = lax.broadcasted_iota(jnp.int32, (HALF, T), 0)
    first = lane < HALF
    eye = jnp.where(lane == row + HALF, 1.0, 0.0).astype(jnp.float32)

    def turn(v):
        return pltpu.roll(v, HALF, 1)

    def tiles(v):
        return [v[8 * i : 8 * i + 8] for i in range(HALF // 8)]

    factor_tiles([tiles(jnp.where(first, a[:HALF], eye)) for a in a_list], r_ref)
    kept, second = [], []
    for m, a in enumerate(a_list):
        r1 = r_ref[m]
        w1 = turn(r1)
        top = dot(w1[:, :HALF], a[:HALF], ((1,), (0,)))
        rest = a[HALF:] - dot(top[:, HALF:], top, ((0,), (0,)))
        kept.append((jnp.where(first, w1, 0.0), top))
        second.append(tiles(jnp.where(first, turn(rest), eye)))
        u_ref[m, :HALF] = jnp.where(first, r1, top)
        w_ref[m, :HALF] = jnp.where(first, w1, 0.0)
    factor_tiles(second, r_ref)
    for m, (w1, top) in enumerate(kept):
        r2 = r_ref[m]
        w2 = turn(r2)
        u_ref[m, HALF:] = jnp.where(first, 0.0, w2)
        low = dot(top[:, HALF:], w1, ((0,), (0,)))
        w_ref[m, HALF:] = jnp.where(first, -dot(w2[:, :HALF], low, ((1,), (0,))), r2)


def tail_kernel(g_ref, b_ref, next_ref, root_ref, iso_ref, adv_ref, s_ref, d_ref, u_ref, w_ref, r_ref):
    count = b_ref.shape[0]
    eye = lax.broadcasted_iota(jnp.int32, (T, T), 0) == lax.broadcasted_iota(jnp.int32, (T, T), 1)
    scales = []
    for m in range(count):
        trace = jnp.zeros((), jnp.float32)
        for n, (p, i) in enumerate(PAIRS):
            for q in range(T // 16):
                s_ref[m, p, i, 16 * q : 16 * q + 16, :] = g_ref[q, m, n]
            if p == i:
                trace = trace + jnp.sum(jnp.where(eye, s_ref[m, p, i], 0.0))
        scales.append(lax.rsqrt(jnp.full((1, T), trace / (NB * T) + 1e-6, jnp.float32)))

    def block(p, carry):
        factor_block([s_ref[m, p, p] for m in range(count)], u_ref, w_ref, r_ref)
        for m in range(count):
            d_ref[m, p] = w_ref[m]
            s_ref[m, p, p] = u_ref[m]

        def panel(i, c):
            for m in range(count):
                s_ref[m, p, i] = dot(w_ref[m], s_ref[m, p, i], ((1,), (0,)))
            return c

        lax.fori_loop(p + 1, NB, panel, 0)

        def trail(i, c):
            def inner(k, c2):
                for m in range(count):
                    s_ref[m, i, k] = s_ref[m, i, k] - dot(s_ref[m, p, i], s_ref[m, p, k], ((0,), (0,)))
                return c2

            return lax.fori_loop(i, NB, inner, c)

        lax.fori_loop(p + 1, NB, trail, 0)
        return carry

    lax.fori_loop(0, NB, block, 0)
    for m in range(count):
        solved = []
        for j in range(NB):
            x = b_ref[m, :, T * j : T * j + T]
            for i in range(j):
                x = x - dot(solved[i], s_ref[m, i, j], ((1,), (0,)))
            x = dot(x, d_ref[m, j], ((1,), (1,)))
            solved.append(x)
            iso_ref[m, :, T * j : T * j + T] = x * root_ref[m, :1, :]
        for p in range(NB):
            total = None
            for i in range(p, NB):
                up = (s_ref[m, p, i] * scales[m]).astype(jnp.bfloat16)
                term = dot(up, next_ref[m, T * i : T * i + T, :], ((1,), (0,)), None)
                total = term if total is None else total + term
            adv_ref[m, T * p : T * p + T, :] = total.astype(jnp.bfloat16)


def tail(gram, bond, next_site, root):
    count, rows, window = bond.shape
    vmem = pl.BlockSpec(memory_space=pltpu.VMEM)
    return pl.pallas_call(
        tail_kernel,
        out_shape=(
            jax.ShapeDtypeStruct((count, rows, window), jnp.float32),
            jax.ShapeDtypeStruct(next_site.shape, jnp.bfloat16),
        ),
        in_specs=[vmem] * 4,
        out_specs=(vmem, vmem),
        scratch_shapes=[
            pltpu.VMEM((count, NB, NB, T, T), jnp.float32),
            pltpu.VMEM((count, NB, T, T), jnp.float32),
            pltpu.VMEM((count, T, T), jnp.float32),
            pltpu.VMEM((count, T, T), jnp.float32),
            pltpu.VMEM((count, HALF, T), jnp.float32),
        ],
        compiler_params=pltpu.CompilerParams(vmem_limit_bytes=40 * 1024 * 1024),
        name="tail",
    )(gram, bond, next_site, root)


CHUNKS = 4
NZ = 8
SIDE = 4
ROWS = 256
MESH = pl.DeviceIdType.MESH
FLOWS = [(0, 0), (1, 1), (0, 1), (1, 0)]


def first_hop(direction, t):
    return 1 if direction == t else 2


def ordered(tasks):
    rate = {"x": 47.0, "y": 47.0, "z": 47.0, "c": 300.0}
    link_free, arrival, done, order = {}, {}, set(), []
    now, left = 0.0, list(tasks)
    while left:
        best = None
        for n, task in enumerate(left):
            if all(a in done for a in task["after"]) and all(k in arrival for k in task["needs"]):
                start = max([now] + [arrival[k] for k in task["needs"]])
                if best is None or start < best[0]:
                    best = (start, n)
        start, n = best
        task = left.pop(n)
        now = start + task["time"]
        for key, link, kib in task["sends"]:
            begin = max(now, link_free.get(link, 0.0))
            link_free[link] = begin + kib / rate[link[0]]
            arrival[key] = link_free[link] + (1.0 if link[0] == "c" else 1.8)
        done.add(task["name"])
        order.append(task)
    return order


def bond_kernel(
    owner_ref, pairs_ref, sizes_ref, charges_ref, env_ref, block_ref, bond_ref, gram_ref, root_ref,
    g0, g1, g2, g3, site_ref, env_v, part, send_b, recv_b, gp, gsend, grecv, gfull,
    env_sem, own_sem, ag_send, ag_recv, rs_send, rs_recv, gr_send, gr_recv, gg_send, gg_recv,
):
    gath = (g0, g1, g2, g3)
    sector, z = lax.axis_index("sector"), lax.axis_index("row")
    c = sector % 2
    x = (sector // 2) % SIDE
    y = sector // (2 * SIDE)

    def at(xx, yy, cc):
        return {"sector": ((yy % SIDE) * SIDE + xx % SIDE) * 2 + cc}

    def along(m, dmaj, dmin):
        return at(x + dmin, y + dmaj, c) if m == 0 else at(x + dmaj, y + dmin, c)

    major, minor = (y, x), (x, y)
    partner = at(x, y, 1 - c)
    up, down = {"row": (z + 1) % NZ}, {"row": (z + NZ - 1) % NZ}

    def slot(m, maj, mino):
        return 32 * m + ((maj % SIDE) * 2 + c) * SIDE + mino % SIDE

    barrier = pltpu.get_barrier_semaphore()
    partners = [along(0, 0, 1), along(0, 0, 3), along(0, 1, 0), along(0, 3, 0), partner, up, down]
    for device in partners:
        pl.semaphore_signal(barrier, inc=1, device_id=device, device_id_type=MESH)
    env_copy = pltpu.make_async_copy(env_ref, env_v, env_sem)
    env_copy.start()
    mine = [2 * sector, 2 * sector + 1]

    def find(n, found):
        return tuple(jnp.where(owner_ref[n] == slot_, n, f) for f, slot_ in zip(found, mine))

    sectors = lax.fori_loop(0, 64, find, (jnp.int32(0), jnp.int32(0)))
    limits, fields, source = [], [], []
    for t in range(2):
        limits.append(sizes_ref[sectors[t]] - z * ROWS)
        fields.append(charges_ref[sectors[t]].astype(jnp.float32) * (2.0 / 64))
        root_ref[t] = jnp.sqrt(jnp.full((8, T), sizes_ref[sectors[t]], jnp.int32).astype(jnp.float32))
        for n in range(4):
            place = owner_ref[pairs_ref[4 * sectors[t] + n]]
            px, py, pc = (place // 4) % SIDE, place // (4 * SIDE), (place // 2) % 2
            even = (py * 2 + pc) * SIDE + px
            odd = 32 + (px * 2 + pc) * SIDE + py
            source.append(jnp.where(place % 2 == 0, even, odd))
    row_ids = lax.broadcasted_iota(jnp.int32, (ROWS, T), 0)
    for j in range(CHUNKS):
        for m in range(2):
            value = block_ref[m, :, T * j : T * j + T].astype(jnp.float32)
            site_ref[j, m] = jnp.where(row_ids < limits[m], value, 0.0).astype(jnp.bfloat16)
    own = []
    for j in range(CHUNKS):
        for m in range(2):
            own.append(
                pltpu.make_async_copy(
                    site_ref.at[j, m], gath[j].at[slot(m, major[m], minor[m])], own_sem.at[j, m]
                )
            )
            own[-1].start()
    pl.semaphore_wait(barrier, len(partners))

    copies = {}

    def send(key, src, dst, ssem, rsem, device):
        copy = pltpu.make_async_remote_copy(
            src_ref=src, dst_ref=dst, send_sem=ssem, recv_sem=rsem, device_id=device, device_id_type=MESH
        )
        copy.start()
        copies[key] = copy

    def ag_send_one(j, m, n, ref, device, src=None):
        send((j, m, n), ref if src is None else src, ref, ag_send.at[j, m, n], ag_recv.at[j, m, n], device)

    def a1(j):
        for m in range(2):
            ref = gath[j].at[slot(m, major[m], minor[m])]
            ag_send_one(j, m, 0, ref, along(m, 0, 1), site_ref.at[j, m])
            ag_send_one(j, m, 1, ref, along(m, 0, 3), site_ref.at[j, m])

    def a2(j):
        for m in range(2):
            copies[j, m, 0].wait_recv()
            low = gath[j].at[slot(m, major[m], minor[m] + 3), pl.ds(0, ROWS // 2)]
            ag_send_one(j, m, 2, low, along(m, 0, 1))
            copies[j, m, 1].wait_recv()
            high = gath[j].at[slot(m, major[m], minor[m] + 1), pl.ds(ROWS // 2, ROWS // 2)]
            ag_send_one(j, m, 3, high, along(m, 0, 3))

    def group(j, m, dmaj, start=0, size=SIDE):
        return gath[j].at[pl.ds(slot(m, major[m] + dmaj, 0) + start, size)]

    def b1(j):
        for m in range(2):
            own[2 * j + m].wait()
            copies[j, m, 2].wait_recv()
            copies[j, m, 3].wait_recv()
            ag_send_one(j, m, 4, group(j, m, 0), along(m, 1, 0))
            ag_send_one(j, m, 5, group(j, m, 0), along(m, 3, 0))
            ag_send_one(j, m, 8, group(j, m, 0), partner)

    def b2(j):
        for m in range(2):
            copies[j, m, 4].wait_recv()
            ag_send_one(j, m, 6, group(j, m, 3, 0, 2), along(m, 1, 0))
            copies[j, m, 5].wait_recv()
            ag_send_one(j, m, 7, group(j, m, 1, 2, 2), along(m, 3, 0))
            ag_send_one(j, m, 9, group(j, m, 3), partner)
            ag_send_one(j, m, 10, group(j, m, 1), partner)

    def b3(j):
        for m in range(2):
            copies[j, m, 6].wait_recv()
            copies[j, m, 7].wait_recv()
            ag_send_one(j, m, 11, group(j, m, 2), partner)

    def ready(j):
        for m in range(2):
            for n in (8, 9, 10, 11):
                copies[j, m, n].wait_recv()
        if j == 0:
            env_copy.wait()

    def multiply(j, r):
        def one(n, carry):
            t = n % 2
            o = (n // 2) * (NZ - 2 * r) + r
            first = pl.multiple_of(((z + o) % NZ) * ROWS, ROWS)
            total = None
            for k in range(4):
                term = jnp.dot(
                    env_v[t, k, pl.ds(first, ROWS), :],
                    gath[j][jnp.where(t == 0, source[k], source[4 + k])],
                    preferred_element_type=jnp.float32,
                )
                total = term if total is None else total + term
            part[j, o, t] = total
            return carry

        lax.fori_loop(0, 2 if r in (0, 4) else 4, one, 0)

    def hop(j, s, direction, t):
        o = 5 - s if direction == 0 else 3 + s
        value = part[j, o, t]
        if s > first_hop(direction, t):
            copies["r", j, s - 1, direction, t].wait_recv()
            value = value + recv_b[j, direction, t, s - 2].astype(jnp.float32)
        send_b[j, direction, t, s - 1] = value.astype(jnp.bfloat16)
        send(
            ("r", j, s, direction, t),
            send_b.at[j, direction, t, s - 1],
            recv_b.at[j, direction, t, s - 1],
            rs_send.at[j, direction, t, s - 1],
            rs_recv.at[j, direction, t, s - 1],
            up if direction == 0 else down,
        )

    def finish(j, t):
        copies["r", j, 4, 0, t].wait_recv()
        copies["r", j, 4, 1, t].wait_recv()
        cols = pl.ds(T * j, T)
        total = part[j, 0, t] + fields[t] * site_ref[j, t].astype(jnp.float32)
        total = total + recv_b[j, 0, t, 3].astype(jnp.float32) + recv_b[j, 1, t, 3].astype(jnp.float32)
        bond_ref[t, :, cols] = jnp.where(row_ids < limits[t], total, 0.0)

    def grams(j):
        for t in range(2):
            for i in range(j + 1):
                value = dot(bond_ref[t, :, T * i : T * i + T], bond_ref[t, :, T * j : T * j + T], ((0,), (0,)))
                for q in range(NZ):
                    gp[j, q, t, i] = value[16 * q : 16 * q + 16]

    def gram_hop(j, s, direction, t):
        o = 5 - s if direction == 0 else 3 + s
        value = gp[j, (z + o) % NZ, t, : j + 1]
        if s > first_hop(direction, t):
            copies["g", j, s - 1, direction, t].wait_recv()
            value = value + grecv[j, direction, t, s - 2, : j + 1]
        gsend[j, direction, t, s - 1, : j + 1] = value
        send(
            ("g", j, s, direction, t),
            gsend.at[j, direction, t, s - 1, pl.ds(0, j + 1)],
            grecv.at[j, direction, t, s - 1, pl.ds(0, j + 1)],
            gr_send.at[j, direction, t, s - 1],
            gr_recv.at[j, direction, t, s - 1],
            up if direction == 0 else down,
        )

    def gram_sum(j, t):
        copies["g", j, 4, 0, t].wait_recv()
        copies["g", j, 4, 1, t].wait_recv()
        total = gp[j, z, t, : j + 1] + grecv[j, 0, t, 3, : j + 1] + grecv[j, 1, t, 3, : j + 1]
        gfull[z, t, j * (j + 1) // 2 : (j + 1) * (j + 2) // 2] = total

    def gram_round(j, s, direction, t):
        if s > 1:
            copies["f", j, s - 1, direction, t].wait_recv()
        q = (z + NZ - (s - 1)) % NZ if direction == 0 else (z + s - 1) % NZ
        piece = gfull.at[q, t, pl.ds(j * (j + 1) // 2, j + 1)]
        send(
            ("f", j, s, direction, t), piece, piece,
            gg_send.at[j, direction, t, s - 1], gg_recv.at[j, direction, t, s - 1],
            up if direction == 0 else down,
        )

    tasks = []

    def task(name, emit, time, needs=(), after=(), sends=()):
        tasks.append(dict(name=name, emit=emit, time=time, needs=needs, after=after, sends=sends))

    def axes(m):
        return ("x", "y") if m == 0 else ("y", "x")

    for j in range(CHUNKS):
        ms = range(2)
        mins, majs = [axes(m)[0] for m in ms], [axes(m)[1] for m in ms]
        task(("a1", j), lambda j=j: a1(j), 0.1,
             after=[] if j == 0 else [("a2", 0)] if j == 1 else [("b1", j - 2)],
             sends=[((j, m, n), mins[m] + str(n), 64) for m in ms for n in (0, 1)])
        task(("a2", j), lambda j=j: a2(j), 0.1, needs=[(j, m, n) for m in ms for n in (0, 1)],
             sends=[((j, m, n + 2), mins[m] + str(n), 32) for m in ms for n in (0, 1)])
        task(("b1", j), lambda j=j: b1(j), 0.1, needs=[(j, m, n) for m in ms for n in (2, 3)],
             after=[("b2", j - 1)] if j else [],
             sends=[((j, m, n + 4), majs[m] + str(n), 256) for m in ms for n in (0, 1)]
             + [((j, m, 8), "c", 256) for m in ms])
        task(("b2", j), lambda j=j: b2(j), 0.1, needs=[(j, m, n) for m in ms for n in (4, 5)],
             sends=[((j, m, n + 6), majs[m] + str(n), 128) for m in ms for n in (0, 1)]
             + [((j, m, n), "c", 256) for m in ms for n in (9, 10)])
        task(("b3", j), lambda j=j: b3(j), 0.1, needs=[(j, m, n) for m in ms for n in (6, 7)],
             sends=[((j, m, 11), "c", 256) for m in ms])
        task(("ready", j), lambda j=j: ready(j), 0.1, needs=[(j, m, n) for m in ms for n in (8, 9, 10, 11)])
        before = ("ready", j)
        for r in (4, 3, 2, 1, 0):
            task(("mm", j, r), lambda j=j, r=r: multiply(j, r), 0.4 if r in (0, 4) else 0.8, after=[before])
            before = ("mm", j, r)
            if r == 0:
                continue
            s = 5 - r
            for direction, t in FLOWS:
                if s >= first_hop(direction, t):
                    more = s > first_hop(direction, t)
                    task(("hop", j, s, direction, t),
                         lambda j=j, s=s, direction=direction, t=t: hop(j, s, direction, t), 0.1,
                         needs=[("r", j, s - 1, direction, t)] if more else [], after=[before],
                         sends=[(("r", j, s, direction, t), "z" + str(direction), 64)])
        for t in range(2):
            task(("finish", j, t), lambda j=j, t=t: finish(j, t), 0.1,
                 needs=[("r", j, 4, 0, t), ("r", j, 4, 1, t)], after=[("mm", j, 0)])
        task(("gram", j), lambda j=j: grams(j), 0.4 + 0.4 * j,
             after=[("finish", j, 0), ("finish", j, 1)] + ([("gram", j - 1)] if j else []))
        for s in range(1, 5):
            for direction, t in FLOWS:
                if s >= first_hop(direction, t):
                    more = s > first_hop(direction, t)
                    task(("ghop", j, s, direction, t),
                         lambda j=j, s=s, direction=direction, t=t: gram_hop(j, s, direction, t), 0.1,
                         needs=[("g", j, s - 1, direction, t)] if more else [], after=[("gram", j)],
                         sends=[(("g", j, s, direction, t), "z" + str(direction), 8 * (j + 1))])
        for t in range(2):
            task(("gsum", j, t), lambda j=j, t=t: gram_sum(j, t), 0.1,
                 needs=[("g", j, 4, 0, t), ("g", j, 4, 1, t)], after=[("gram", j)])
        for s in range(1, 5):
            for direction, t in FLOWS:
                if s < 4 or direction == t:
                    task(("ground", j, s, direction, t),
                         lambda j=j, s=s, direction=direction, t=t: gram_round(j, s, direction, t), 0.1,
                         needs=[("f", j, s - 1, direction, t)] if s > 1 else [], after=[("gsum", j, t)],
                         sends=[(("f", j, s, direction, t), "z" + str(direction), 8 * (j + 1))])
    for item in ordered(tasks):
        item["emit"]()
    for j in range(CHUNKS):
        for direction, t in FLOWS:
            copies["f", j, 4 if direction == t else 3, direction, t].wait_recv()
    for copy in copies.values():
        copy.wait_send()
    gram_ref[...] = gfull[...]


def bond_and_gram(owner, pairs, sizes, charges, environment, site_block):
    vmem, anywhere = pl.BlockSpec(memory_space=pltpu.VMEM), pl.BlockSpec(memory_space=pl.ANY)
    bf, f32 = jnp.bfloat16, jnp.float32
    dma = pltpu.SemaphoreType.DMA
    blocks = len(PAIRS)
    return pl.pallas_call(
        bond_kernel,
        out_shape=(
            jax.ShapeDtypeStruct(site_block.shape, f32),
            jax.ShapeDtypeStruct((NZ, 2, blocks, 16, T), f32),
            jax.ShapeDtypeStruct((2, 8, T), f32),
        ),
        in_specs=[pl.BlockSpec(memory_space=pltpu.SMEM)] * 4 + [anywhere, vmem],
        out_specs=(vmem, vmem, vmem),
        scratch_shapes=[pltpu.VMEM((64, ROWS, T), bf)] * CHUNKS
        + [
            pltpu.VMEM((CHUNKS, 2, ROWS, T), bf),
            pltpu.VMEM(environment.shape, bf),
            pltpu.VMEM((CHUNKS, NZ, 2, ROWS, T), f32),
            pltpu.VMEM((CHUNKS, 2, 2, 4, ROWS, T), bf),
            pltpu.VMEM((CHUNKS, 2, 2, 4, ROWS, T), bf),
            pltpu.VMEM((CHUNKS, NZ, 2, NB, 16, T), f32),
            pltpu.VMEM((CHUNKS, 2, 2, 4, NB, 16, T), f32),
            pltpu.VMEM((CHUNKS, 2, 2, 4, NB, 16, T), f32),
            pltpu.VMEM((NZ, 2, blocks, 16, T), f32),
            dma,
            dma((CHUNKS, 2)),
            dma((CHUNKS, 2, 12)),
            dma((CHUNKS, 2, 12)),
            dma((CHUNKS, 2, 2, 4)),
            dma((CHUNKS, 2, 2, 4)),
            dma((CHUNKS, 2, 2, 4)),
            dma((CHUNKS, 2, 2, 4)),
            dma((CHUNKS, 2, 2, 4)),
            dma((CHUNKS, 2, 2, 4)),
        ],
        compiler_params=pltpu.CompilerParams(
            vmem_limit_bytes=62 * 1024 * 1024, collective_id=0, has_side_effects=True
        ),
        name="bond",
    )(owner, pairs, sizes, charges, environment, site_block)


def local(environment, site_block, next_site, charges, sizes, pairs, owner):
    bond, gram, root = bond_and_gram(owner, pairs.reshape(-1), sizes, charges, environment, site_block)
    iso, advanced = tail(gram, bond, next_site, root)
    return (jnp.swapaxes(iso, 0, 1), advanced)


def solution(mesh):
    return jax.shard_map(
        local,
        mesh=mesh,
        in_specs=(
            P("sector", None, None, "row"),
            P("sector", "row", None),
            P("sector", None, "row"),
            P(),
            P(),
            P(),
            P(),
        ),
        out_specs=(P("row", "sector", None), P("sector", None, "row")),
        check_vma=False,
    )
```

```python
import jax
import jax.numpy as jnp
from jax import lax
from jax.experimental import pallas as pl
from jax.experimental.pallas import tpu as pltpu
from jax.sharding import PartitionSpec as P

NB = 4
T = 128
GROUP = 8
HALF = 64
HI = lax.Precision.HIGHEST


def dot(a, b, dims, precision=HI):
    return lax.dot_general(
        a, b, (dims, ((), ())), precision=precision, preferred_element_type=jnp.float32
    )


def factor_tiles(a_tiles, r_ref):
    count = len(a_tiles)
    rows8 = HALF // 8
    lane = lax.broadcasted_iota(jnp.int32, (8, T), 1)
    sub = lax.broadcasted_iota(jnp.int32, (8, T), 0)

    def spread(x, s):
        return jnp.broadcast_to(x[s : s + 1, :], (8, T))

    for j0 in range(0, HALF, GROUP):
        g = j0 // 8
        s0 = j0 - 8 * g
        state = []
        for m in range(count):
            cols = [
                [
                    jnp.broadcast_to(a_tiles[m][i][:, j0 + k : j0 + k + 1], (8, T))
                    for i in range(g, rows8)
                ]
                for k in range(GROUP)
            ]
            rows = [spread(a_tiles[m][g], s0 + k) for k in range(GROUP)]
            state.append((cols, rows))
        for k in range(GROUP):
            for m in range(count):
                cols, rows = state[m]
                rs = lax.rsqrt(spread(cols[k][0], s0 + k))
                cols[k] = [c * rs for c in cols[k]]
                rows[k] = rows[k] * rs
                for q in range(k + 1, GROUP):
                    f = spread(cols[k][0], s0 + q)
                    cols[q] = [c - l * f for c, l in zip(cols[q], cols[k])]
                    rows[q] = rows[q] - rows[k] * f
        for m in range(count):
            cols, rows = state[m]
            for k in range(GROUP):
                j = j0 + k
                r_ref[m, j : j + 1, :] = jnp.where(lane[:1] >= j, rows[k][:1], 0.0)
            last = s0 + GROUP == 8
            for i in range(g + 1 if last else g, rows8):
                a = a_tiles[m][i]
                for k in range(GROUP):
                    l = cols[k][i - g]
                    if i == g:
                        l = jnp.where(sub >= s0 + GROUP, l, 0.0)
                    a = a - l * rows[k]
                a_tiles[m][i] = a


def factor_block(a_list, u_ref, w_ref, r_ref, between):
    lane = lax.broadcasted_iota(jnp.int32, (HALF, T), 1)
    row = lax.broadcasted_iota(jnp.int32, (HALF, T), 0)
    first = lane < HALF
    eye = jnp.where(lane == row + HALF, 1.0, 0.0).astype(jnp.float32)

    def turn(v):
        return pltpu.roll(v, HALF, 1)

    def tiles(v):
        return [v[8 * i : 8 * i + 8] for i in range(HALF // 8)]

    factor_tiles([tiles(jnp.where(first, a[:HALF], eye)) for a in a_list], r_ref)
    kept, second = [], []
    for m, a in enumerate(a_list):
        r1 = r_ref[m]
        w1 = turn(r1)
        top = dot(w1[:, :HALF], a[:HALF], ((1,), (0,)))
        rest = a[HALF:] - dot(top[:, HALF:], top, ((0,), (0,)))
        kept.append((jnp.where(first, w1, 0.0), top))
        second.append(tiles(jnp.where(first, turn(rest), eye)))
        u_ref[m, :HALF] = jnp.where(first, r1, top)
        w_ref[m, :HALF] = jnp.where(first, w1, 0.0)
    between()
    factor_tiles(second, r_ref)
    for m, (w1, top) in enumerate(kept):
        r2 = r_ref[m]
        w2 = turn(r2)
        u_ref[m, HALF:] = jnp.where(first, 0.0, w2)
        low = dot(top[:, HALF:], w1, ((0,), (0,)))
        w_ref[m, HALF:] = jnp.where(first, -dot(w2[:, :HALF], low, ((1,), (0,))), r2)


CHUNKS = 4
NZ = 8
SIDE = 4
ROWS = 256
MESH = pl.DeviceIdType.MESH
FLOWS = [(0, 0), (1, 1), (0, 1), (1, 0)]


def first_hop(direction, t):
    return 1 if direction == t else 2


def ordered(tasks):
    rate = {"x": 43.0, "y": 43.0, "z": 43.0, "c": 300.0}
    link_free, arrival, done, order = {}, {}, set(), []
    now, left = 0.0, list(tasks)
    while left:
        best = None
        for n, task in enumerate(left):
            if all(a in done for a in task["after"]) and all(k in arrival for k in task["needs"]):
                start = max([now] + [arrival[k] for k in task["needs"]])
                if best is None or start < best[0]:
                    best = (start, n)
        start, n = best
        task = left.pop(n)
        now = start + task["time"]
        for key, link, kib in task["sends"]:
            begin = max(now, link_free.get(link, 0.0))
            link_free[link] = begin + kib / rate[link[0]]
            arrival[key] = link_free[link] + (1.0 if link[0] == "c" else 1.8)
        done.add(task["name"])
        order.append(task)
    return order


def bond_kernel(
    owner_ref, pairs_ref, sizes_ref, charges_ref, env_ref, block_ref, next_hbm, iso_ref, adv_ref,
    g0, g1, g2, g3, site_ref, env_v, part, send_b, recv_b, gp, gsend, grecv, gfull,
    bond_ref, root_ref, next_ref, s_ref, d_ref, u_ref, w_ref, r_ref,
    env_sem, next_sem, own_sem, ag_send, ag_recv, rs_send, rs_recv, gr_send, gr_recv, gg_send, gg_recv,
):
    gath = (g0, g1, g2, g3)
    sector, z = lax.axis_index("sector"), lax.axis_index("row")
    c = sector % 2
    x = (sector // 2) % SIDE
    y = sector // (2 * SIDE)

    def at(xx, yy, cc):
        return {"sector": ((yy % SIDE) * SIDE + xx % SIDE) * 2 + cc}

    def along(m, dmaj, dmin):
        return at(x + dmin, y + dmaj, c) if m == 0 else at(x + dmaj, y + dmin, c)

    major, minor = (y, x), (x, y)
    partner = at(x, y, 1 - c)
    up, down = {"row": (z + 1) % NZ}, {"row": (z + NZ - 1) % NZ}

    def slot(m, maj, mino):
        return 32 * m + ((maj % SIDE) * 2 + c) * SIDE + mino % SIDE

    barrier = pltpu.get_barrier_semaphore()
    partners = [along(0, 0, 1), along(0, 0, 3), along(0, 1, 0), along(0, 3, 0), partner, up, down]
    for device in partners:
        pl.semaphore_signal(barrier, inc=1, device_id=device, device_id_type=MESH)
    env_copy = pltpu.make_async_copy(env_ref, env_v, env_sem)
    env_copy.start()
    next_copy = pltpu.make_async_copy(next_hbm, next_ref, next_sem)
    next_copy.start()
    mine = [2 * sector, 2 * sector + 1]

    def find(n, found):
        return tuple(jnp.where(owner_ref[n] == slot_, n, f) for f, slot_ in zip(found, mine))

    sectors = lax.fori_loop(0, 64, find, (jnp.int32(0), jnp.int32(0)))
    limits, fields, source = [], [], []
    for t in range(2):
        limits.append(sizes_ref[sectors[t]] - z * ROWS)
        fields.append(charges_ref[sectors[t]].astype(jnp.float32) * (2.0 / 64))
        root_ref[t] = jnp.sqrt(jnp.full((8, T), sizes_ref[sectors[t]], jnp.int32).astype(jnp.float32))
        for n in range(4):
            place = owner_ref[pairs_ref[4 * sectors[t] + n]]
            px, py, pc = (place // 4) % SIDE, place // (4 * SIDE), (place // 2) % 2
            even = (py * 2 + pc) * SIDE + px
            odd = 32 + (px * 2 + pc) * SIDE + py
            source.append(jnp.where(place % 2 == 0, even, odd))
    row_ids = lax.broadcasted_iota(jnp.int32, (ROWS, T), 0)
    for j in range(CHUNKS):
        for m in range(2):
            value = block_ref[m, :, T * j : T * j + T].astype(jnp.float32)
            site_ref[j, m] = jnp.where(row_ids < limits[m], value, 0.0).astype(jnp.bfloat16)
    own = []
    for j in range(CHUNKS):
        for m in range(2):
            own.append(
                pltpu.make_async_copy(
                    site_ref.at[j, m], gath[j].at[slot(m, major[m], minor[m])], own_sem.at[j, m]
                )
            )
            own[-1].start()
    pl.semaphore_wait(barrier, len(partners))

    copies = {}

    def send(key, src, dst, ssem, rsem, device, late=False):
        copy = pltpu.make_async_remote_copy(
            src_ref=src, dst_ref=dst, send_sem=ssem, recv_sem=rsem, device_id=device, device_id_type=MESH
        )
        copies[key] = copy
        if not late:
            copy.start()

    def ag_send_one(j, m, n, ref, device, src=None):
        send((j, m, n), ref if src is None else src, ref, ag_send.at[j, m, n], ag_recv.at[j, m, n], device)

    def a1(j):
        for m in range(2):
            ref = gath[j].at[slot(m, major[m], minor[m])]
            ag_send_one(j, m, 0, ref, along(m, 0, 1), site_ref.at[j, m])
            ag_send_one(j, m, 1, ref, along(m, 0, 3), site_ref.at[j, m])

    def a2(j):
        for m in range(2):
            copies[j, m, 0].wait_recv()
            low = gath[j].at[slot(m, major[m], minor[m] + 3), pl.ds(0, ROWS // 2)]
            ag_send_one(j, m, 2, low, along(m, 0, 1))
            copies[j, m, 1].wait_recv()
            high = gath[j].at[slot(m, major[m], minor[m] + 1), pl.ds(ROWS // 2, ROWS // 2)]
            ag_send_one(j, m, 3, high, along(m, 0, 3))

    def group(j, m, dmaj, start=0, size=SIDE):
        return gath[j].at[pl.ds(slot(m, major[m] + dmaj, 0) + start, size)]

    def b1(j):
        for m in range(2):
            own[2 * j + m].wait()
            copies[j, m, 2].wait_recv()
            copies[j, m, 3].wait_recv()
            ag_send_one(j, m, 4, group(j, m, 0), along(m, 1, 0))
            ag_send_one(j, m, 5, group(j, m, 0), along(m, 3, 0))
            ag_send_one(j, m, 8, group(j, m, 0), partner)

    def b2(j):
        for m in range(2):
            copies[j, m, 4].wait_recv()
            ag_send_one(j, m, 6, group(j, m, 3, 0, 2), along(m, 1, 0))
            copies[j, m, 5].wait_recv()
            ag_send_one(j, m, 7, group(j, m, 1, 2, 2), along(m, 3, 0))
            ag_send_one(j, m, 9, group(j, m, 3), partner)
            ag_send_one(j, m, 10, group(j, m, 1), partner)

    def b3(j):
        for m in range(2):
            copies[j, m, 6].wait_recv()
            copies[j, m, 7].wait_recv()
            ag_send_one(j, m, 11, group(j, m, 2), partner)

    def ready(j):
        for m in range(2):
            for n in (8, 9, 10, 11):
                copies[j, m, n].wait_recv()
        if j == 0:
            env_copy.wait()

    def multiply(j, r):
        def one(n, carry):
            t = n % 2
            o = (n // 2) * (NZ - 2 * r) + r
            first = pl.multiple_of(((z + o) % NZ) * ROWS, ROWS)
            total = None
            for k in range(4):
                term = jnp.dot(
                    env_v[t, k, pl.ds(first, ROWS), :],
                    gath[j][jnp.where(t == 0, source[k], source[4 + k])],
                    preferred_element_type=jnp.float32,
                )
                total = term if total is None else total + term
            part[j, o, t] = total
            return carry

        lax.fori_loop(0, 2 if r in (0, 4) else 4, one, 0)

    def hop(j, s, direction, t):
        o = 5 - s if direction == 0 else 3 + s
        value = part[j, o, t]
        if s > first_hop(direction, t):
            copies["r", j, s - 1, direction, t].wait_recv()
            value = value + recv_b[j, direction, t, s - 2].astype(jnp.float32)
        send_b[j, direction, t, s - 1] = value.astype(jnp.bfloat16)
        send(
            ("r", j, s, direction, t),
            send_b.at[j, direction, t, s - 1],
            recv_b.at[j, direction, t, s - 1],
            rs_send.at[j, direction, t, s - 1],
            rs_recv.at[j, direction, t, s - 1],
            up if direction == 0 else down,
        )

    def finish(j, t):
        copies["r", j, 4, 0, t].wait_recv()
        copies["r", j, 4, 1, t].wait_recv()
        cols = pl.ds(T * j, T)
        total = part[j, 0, t] + fields[t] * site_ref[j, t].astype(jnp.float32)
        total = total + recv_b[j, 0, t, 3].astype(jnp.float32) + recv_b[j, 1, t, 3].astype(jnp.float32)
        bond_ref[t, :, cols] = jnp.where(row_ids < limits[t], total, 0.0)

    def grams(j):
        for t in range(2):
            for i in range(j + 1):
                value = dot(bond_ref[t, :, T * i : T * i + T], bond_ref[t, :, T * j : T * j + T], ((0,), (0,)))
                for q in range(NZ):
                    gp[j, q, t, i] = value[16 * q : 16 * q + 16]

    for j in range(CHUNKS):
        for s in range(1, 5):
            for direction, t in FLOWS:
                device = up if direction == 0 else down
                if s >= first_hop(direction, t):
                    send(
                        ("g", j, s, direction, t),
                        gsend.at[j, direction, t, s - 1, pl.ds(0, j + 1)],
                        grecv.at[j, direction, t, s - 1, pl.ds(0, j + 1)],
                        gr_send.at[j, direction, t, s - 1],
                        gr_recv.at[j, direction, t, s - 1],
                        device, late=True,
                    )
                if s < 4 or direction == t:
                    q = (z + NZ - (s - 1)) % NZ if direction == 0 else (z + s - 1) % NZ
                    piece = gfull.at[q, t, pl.ds(j * (j + 1) // 2, j + 1)]
                    send(
                        ("f", j, s, direction, t), piece, piece,
                        gg_send.at[j, direction, t, s - 1], gg_recv.at[j, direction, t, s - 1],
                        device, late=True,
                    )

    def gram_hop(j, s, direction, t):
        o = 5 - s if direction == 0 else 3 + s
        value = gp[j, (z + o) % NZ, t, : j + 1]
        if s > first_hop(direction, t):
            copies["g", j, s - 1, direction, t].wait_recv()
            value = value + grecv[j, direction, t, s - 2, : j + 1]
        gsend[j, direction, t, s - 1, : j + 1] = value
        copies["g", j, s, direction, t].start()

    def gram_sum(j, t):
        copies["g", j, 4, 0, t].wait_recv()
        copies["g", j, 4, 1, t].wait_recv()
        total = gp[j, z, t, : j + 1] + grecv[j, 0, t, 3, : j + 1] + grecv[j, 1, t, 3, : j + 1]
        gfull[z, t, j * (j + 1) // 2 : (j + 1) * (j + 2) // 2] = total

    def gram_round(j, s, direction, t):
        if s > 1:
            copies["f", j, s - 1, direction, t].wait_recv()
        copies["f", j, s, direction, t].start()

    def hops(j, s):
        for direction, t in FLOWS:
            if s >= first_hop(direction, t):
                gram_hop(j, s, direction, t)

    def sums(j):
        for t in range(2):
            gram_sum(j, t)

    def rounds(j, s):
        for direction, t in FLOWS:
            if s < 4 or direction == t:
                gram_round(j, s, direction, t)

    def last(j):
        for direction, t in FLOWS:
            copies["f", j, 4 if direction == t else 3, direction, t].wait_recv()
        for i in range(j + 1):
            for m in range(2):
                for q in range(NZ):
                    s_ref[m, i, j, 16 * q : 16 * q + 16, :] = gfull[q, m, j * (j + 1) // 2 + i]

    late_steps = {
        (0, 0): lambda: (last(0), hops(3, 1)),
        (0, 1): lambda: (sums(2), rounds(2, 1), hops(3, 2)),
        (0, 2): lambda: (rounds(2, 2), hops(3, 3)),
        (1, 0): lambda: (last(1), rounds(2, 3), hops(3, 4)),
        (1, 1): lambda: (rounds(2, 4), sums(3), rounds(3, 1)),
        (1, 2): lambda: rounds(3, 2),
        (2, 0): lambda: (last(2), rounds(3, 3)),
        (2, 1): lambda: rounds(3, 4),
        (3, 0): lambda: last(3),
    }

    def point(p, n):
        for (block, place), run in late_steps.items():
            if place == n:

                @pl.when(p == block)
                def _(run=run):
                    run()

    tasks = []

    def task(name, emit, time, needs=(), after=(), sends=()):
        tasks.append(dict(name=name, emit=emit, time=time, needs=needs, after=after, sends=sends))

    def axes(m):
        return ("x", "y") if m == 0 else ("y", "x")

    for j in range(CHUNKS):
        ms = range(2)
        mins, majs = [axes(m)[0] for m in ms], [axes(m)[1] for m in ms]
        task(("a1", j), lambda j=j: a1(j), 0.1,
             after=[] if j == 0 else [("a2", 0)] if j == 1 else [("b1", j - 2)],
             sends=[((j, m, n), mins[m] + str(n), 64) for m in ms for n in (0, 1)])
        task(("a2", j), lambda j=j: a2(j), 0.1, needs=[(j, m, n) for m in ms for n in (0, 1)],
             sends=[((j, m, n + 2), mins[m] + str(n), 32) for m in ms for n in (0, 1)])
        task(("b1", j), lambda j=j: b1(j), 0.1, needs=[(j, m, n) for m in ms for n in (2, 3)],
             after=[("b2", j - 1)] if j else [],
             sends=[((j, m, n + 4), majs[m] + str(n), 256) for m in ms for n in (0, 1)]
             + [((j, m, 8), "c", 256) for m in ms])
        task(("b2", j), lambda j=j: b2(j), 0.1, needs=[(j, m, n) for m in ms for n in (4, 5)],
             sends=[((j, m, n + 6), majs[m] + str(n), 128) for m in ms for n in (0, 1)]
             + [((j, m, n), "c", 256) for m in ms for n in (9, 10)])
        task(("b3", j), lambda j=j: b3(j), 0.1, needs=[(j, m, n) for m in ms for n in (6, 7)],
             sends=[((j, m, 11), "c", 256) for m in ms])
        task(("ready", j), lambda j=j: ready(j), 0.1, needs=[(j, m, n) for m in ms for n in (8, 9, 10, 11)])
        before = ("ready", j)
        for r in (4, 3, 2, 1, 0):
            task(("mm", j, r), lambda j=j, r=r: multiply(j, r), 0.4 if r in (0, 4) else 0.8, after=[before])
            before = ("mm", j, r)
            if r == 0:
                continue
            s = 5 - r
            for direction, t in FLOWS:
                if s >= first_hop(direction, t):
                    more = s > first_hop(direction, t)
                    task(("hop", j, s, direction, t),
                         lambda j=j, s=s, direction=direction, t=t: hop(j, s, direction, t), 0.1,
                         needs=[("r", j, s - 1, direction, t)] if more else [], after=[before],
                         sends=[(("r", j, s, direction, t), "z" + str(direction), 64)])
        for t in range(2):
            task(("finish", j, t), lambda j=j, t=t: finish(j, t), 0.1,
                 needs=[("r", j, 4, 0, t), ("r", j, 4, 1, t)], after=[("mm", j, 0)])
        task(("gram", j), lambda j=j: grams(j), 0.4 + 0.4 * j,
             after=[("finish", j, 0), ("finish", j, 1)] + ([("gram", j - 1)] if j else []))
        for s in range(1, 5):
            for direction, t in FLOWS:
                if s >= first_hop(direction, t) and j < 3:
                    more = s > first_hop(direction, t)
                    task(("ghop", j, s, direction, t),
                         lambda j=j, s=s, direction=direction, t=t: gram_hop(j, s, direction, t), 0.1,
                         needs=[("g", j, s - 1, direction, t)] if more else [], after=[("gram", j)],
                         sends=[(("g", j, s, direction, t), "z" + str(direction), 8 * (j + 1))])
        for t in range(2 if j < 2 else 0):
            task(("gsum", j, t), lambda j=j, t=t: gram_sum(j, t), 0.1,
                 needs=[("g", j, 4, 0, t), ("g", j, 4, 1, t)], after=[("gram", j)])
        for s in range(1, 5):
            for direction, t in FLOWS:
                if j < 2 and (s < 4 or direction == t):
                    task(("ground", j, s, direction, t),
                         lambda j=j, s=s, direction=direction, t=t: gram_round(j, s, direction, t), 0.1,
                         needs=[("f", j, s - 1, direction, t)] if s > 1 else [], after=[("gsum", j, t)],
                         sends=[(("f", j, s, direction, t), "z" + str(direction), 8 * (j + 1))])
    for item in ordered(tasks):
        item["emit"]()

    def block(p, carry):
        point(p, 0)
        def column(i, c):
            def above(k, c2):
                for m in range(2):
                    s_ref[m, i, p] = s_ref[m, i, p] - dot(s_ref[m, k, i], s_ref[m, k, p], ((0,), (0,)))
                return c2

            lax.fori_loop(0, i, above, 0)
            for m in range(2):
                value = dot(d_ref[m, i], s_ref[m, i, p], ((1,), (0,)))
                s_ref[m, i, p] = value
                s_ref[m, p, p] = s_ref[m, p, p] - dot(value, value, ((0,), (0,)))
            return c

        lax.fori_loop(0, p, column, 0)
        factor_block([s_ref[m, p, p] for m in range(2)], u_ref, w_ref, r_ref, lambda: point(p, 1))
        for m in range(2):
            d_ref[m, p] = w_ref[m]
            s_ref[m, p, p] = u_ref[m]
        point(p, 2)
        return carry

    lax.fori_loop(0, NB, block, 0)
    next_copy.wait()
    row16 = lax.broadcasted_iota(jnp.int32, (16, T), 0)
    lane16 = lax.broadcasted_iota(jnp.int32, (16, T), 1)
    for m in range(2):
        trace = jnp.zeros((16, T), jnp.float32)
        for p in range(NB):
            for q in range(NZ):
                trace = trace + jnp.where(lane16 == row16 + 16 * q, gfull[q, m, p * (p + 3) // 2], 0.0)
        scale = lax.rsqrt(jnp.full((1, T), jnp.sum(trace) / (NB * T) + 1e-6, jnp.float32))
        solved = []
        for j in range(NB):
            value = bond_ref[m, :, T * j : T * j + T]
            for i in range(j):
                value = value - dot(solved[i], s_ref[m, i, j], ((1,), (0,)))
            value = dot(value, d_ref[m, j], ((1,), (1,)))
            solved.append(value)
            iso_ref[m, :, T * j : T * j + T] = value * root_ref[m, :1, :]
        for p in range(NB):
            total = None
            for i in range(p, NB):
                up_block = (s_ref[m, p, i] * scale).astype(jnp.bfloat16)
                term = dot(up_block, next_ref[m, T * i : T * i + T, :], ((1,), (0,)), None)
                total = term if total is None else total + term
            adv_ref[m, T * p : T * p + T, :] = total.astype(jnp.bfloat16)
    for copy in copies.values():
        copy.wait_send()


def site_step(owner, pairs, sizes, charges, environment, site_block, next_site):
    vmem, anywhere = pl.BlockSpec(memory_space=pltpu.VMEM), pl.BlockSpec(memory_space=pl.ANY)
    bf, f32 = jnp.bfloat16, jnp.float32
    dma = pltpu.SemaphoreType.DMA
    blocks = NB * (NB + 1) // 2
    return pl.pallas_call(
        bond_kernel,
        out_shape=(
            jax.ShapeDtypeStruct(site_block.shape, f32),
            jax.ShapeDtypeStruct(next_site.shape, bf),
        ),
        in_specs=[pl.BlockSpec(memory_space=pltpu.SMEM)] * 4 + [anywhere, vmem, anywhere],
        out_specs=(vmem, vmem),
        scratch_shapes=[pltpu.VMEM((64, ROWS, T), bf)] * CHUNKS
        + [
            pltpu.VMEM((CHUNKS, 2, ROWS, T), bf),
            pltpu.VMEM(environment.shape, bf),
            pltpu.VMEM((CHUNKS, NZ, 2, ROWS, T), f32),
            pltpu.VMEM((CHUNKS, 2, 2, 4, ROWS, T), bf),
            pltpu.VMEM((CHUNKS, 2, 2, 4, ROWS, T), bf),
            pltpu.VMEM((CHUNKS, NZ, 2, NB, 16, T), f32),
            pltpu.VMEM((CHUNKS, 2, 2, 4, NB, 16, T), f32),
            pltpu.VMEM((CHUNKS, 2, 2, 4, NB, 16, T), f32),
            pltpu.VMEM((NZ, 2, blocks, 16, T), f32),
            pltpu.VMEM(site_block.shape, f32),
            pltpu.VMEM((2, 8, T), f32),
            pltpu.VMEM(next_site.shape, bf),
            pltpu.VMEM((2, NB, NB, T, T), f32),
            pltpu.VMEM((2, NB, T, T), f32),
            pltpu.VMEM((2, T, T), f32),
            pltpu.VMEM((2, T, T), f32),
            pltpu.VMEM((2, HALF, T), f32),
            dma,
            dma,
            dma((CHUNKS, 2)),
            dma((CHUNKS, 2, 12)),
            dma((CHUNKS, 2, 12)),
            dma((CHUNKS, 2, 2, 4)),
            dma((CHUNKS, 2, 2, 4)),
            dma((CHUNKS, 2, 2, 4)),
            dma((CHUNKS, 2, 2, 4)),
            dma((CHUNKS, 2, 2, 4)),
            dma((CHUNKS, 2, 2, 4)),
        ],
        compiler_params=pltpu.CompilerParams(
            vmem_limit_bytes=63 * 1024 * 1024, collective_id=0, has_side_effects=True
        ),
        name="bond",
    )(owner, pairs, sizes, charges, environment, site_block, next_site)


def local(environment, site_block, next_site, charges, sizes, pairs, owner):
    iso, advanced = site_step(
        owner, pairs.reshape(-1), sizes, charges, environment, site_block, next_site
    )
    return (jnp.swapaxes(iso, 0, 1), advanced)


def solution(mesh):
    return jax.shard_map(
        local,
        mesh=mesh,
        in_specs=(
            P("sector", None, None, "row"),
            P("sector", "row", None),
            P("sector", None, "row"),
            P(),
            P(),
            P(),
            P(),
        ),
        out_specs=(P("row", "sector", None), P("sector", None, "row")),
        check_vma=False,
    )
```

```python
import jax
import jax.numpy as jnp
from jax import lax
from jax.experimental import pallas as pl
from jax.experimental.pallas import tpu as pltpu
from jax.sharding import PartitionSpec as P

NB = 4
T = 128
GROUP = 8
HALF = 64
HI = lax.Precision.HIGHEST


def dot(a, b, dims, precision=HI):
    return lax.dot_general(
        a, b, (dims, ((), ())), precision=precision, preferred_element_type=jnp.float32
    )


def factor_tiles(a_tiles, r_ref):
    count = len(a_tiles)
    rows8 = HALF // 8
    lane = lax.broadcasted_iota(jnp.int32, (8, T), 1)
    sub = lax.broadcasted_iota(jnp.int32, (8, T), 0)

    def spread(x, s):
        return jnp.broadcast_to(x[s : s + 1, :], (8, T))

    for j0 in range(0, HALF, GROUP):
        g = j0 // 8
        s0 = j0 - 8 * g
        state = []
        for m in range(count):
            cols = [
                [
                    jnp.broadcast_to(a_tiles[m][i][:, j0 + k : j0 + k + 1], (8, T))
                    for i in range(g, rows8)
                ]
                for k in range(GROUP)
            ]
            rows = [spread(a_tiles[m][g], s0 + k) for k in range(GROUP)]
            state.append((cols, rows))
        for k in range(GROUP):
            for m in range(count):
                cols, rows = state[m]
                rs = lax.rsqrt(spread(cols[k][0], s0 + k))
                cols[k] = [c * rs for c in cols[k]]
                rows[k] = rows[k] * rs
                for q in range(k + 1, GROUP):
                    f = spread(cols[k][0], s0 + q)
                    cols[q] = [c - l * f for c, l in zip(cols[q], cols[k])]
                    rows[q] = rows[q] - rows[k] * f
        for m in range(count):
            cols, rows = state[m]
            for k in range(GROUP):
                j = j0 + k
                r_ref[m, j : j + 1, :] = jnp.where(lane[:1] >= j, rows[k][:1], 0.0)
            last = s0 + GROUP == 8
            for i in range(g + 1 if last else g, rows8):
                a = a_tiles[m][i]
                for k in range(GROUP):
                    l = cols[k][i - g]
                    if i == g:
                        l = jnp.where(sub >= s0 + GROUP, l, 0.0)
                    a = a - l * rows[k]
                a_tiles[m][i] = a


def factor_block(a_list, u_ref, w_ref, r_ref, between):
    lane = lax.broadcasted_iota(jnp.int32, (HALF, T), 1)
    row = lax.broadcasted_iota(jnp.int32, (HALF, T), 0)
    first = lane < HALF
    eye = jnp.where(lane == row + HALF, 1.0, 0.0).astype(jnp.float32)

    def turn(v):
        return pltpu.roll(v, HALF, 1)

    def tiles(v):
        return [v[8 * i : 8 * i + 8] for i in range(HALF // 8)]

    factor_tiles([tiles(jnp.where(first, a[:HALF], eye)) for a in a_list], r_ref)
    kept, second = [], []
    for m, a in enumerate(a_list):
        r1 = r_ref[m]
        w1 = turn(r1)
        top = dot(w1[:, :HALF], a[:HALF], ((1,), (0,)))
        rest = a[HALF:] - dot(top[:, HALF:], top, ((0,), (0,)))
        kept.append((jnp.where(first, w1, 0.0), top))
        second.append(tiles(jnp.where(first, turn(rest), eye)))
        u_ref[m, :HALF] = jnp.where(first, r1, top)
        w_ref[m, :HALF] = jnp.where(first, w1, 0.0)
    between()
    factor_tiles(second, r_ref)
    for m, (w1, top) in enumerate(kept):
        r2 = r_ref[m]
        w2 = turn(r2)
        u_ref[m, HALF:] = jnp.where(first, 0.0, w2)
        low = dot(top[:, HALF:], w1, ((0,), (0,)))
        w_ref[m, HALF:] = jnp.where(first, -dot(w2[:, :HALF], low, ((1,), (0,))), r2)


CHUNKS = 4
NZ = 8
SIDE = 4
ROWS = 256
MESH = pl.DeviceIdType.MESH
FLOWS = [(0, 0), (1, 1), (0, 1), (1, 0)]


def first_hop(direction, t):
    return 1 if direction == t else 2


def ordered(tasks):
    rate = {"x": 43.0, "y": 43.0, "z": 43.0, "c": 300.0}
    link_free, arrival, done, order = {}, {}, set(), []
    now, left = 0.0, list(tasks)
    while left:
        best = None
        for n, task in enumerate(left):
            if all(a in done for a in task["after"]) and all(k in arrival for k in task["needs"]):
                start = max([now] + [arrival[k] for k in task["needs"]])
                if best is None or start < best[0]:
                    best = (start, n)
        start, n = best
        task = left.pop(n)
        now = start + task["time"]
        for key, link, kib in task["sends"]:
            begin = max(now, link_free.get(link, 0.0))
            link_free[link] = begin + kib / rate[link[0]]
            arrival[key] = link_free[link] + (1.0 if link[0] == "c" else 1.8)
        done.add(task["name"])
        order.append(task)
    return order


def bond_kernel(
    owner_ref, pairs_ref, sizes_ref, charges_ref, env_ref, block_ref, next_hbm, iso_ref, adv_ref,
    g0, g1, g2, g3, site_ref, env_v, part, send_b, recv_b, gp, gsend, grecv, gfull,
    bond_ref, root_ref, next_ref, s_ref, d_ref, u_ref, w_ref, r_ref,
    env_sem, next_sem, own_sem, ag_send, ag_recv, rs_send, rs_recv, gr_send, gr_recv, gg_send, gg_recv,
):
    gath = (g0, g1, g2, g3)
    sector, z = lax.axis_index("sector"), lax.axis_index("row")
    c = sector % 2
    x = (sector // 2) % SIDE
    y = sector // (2 * SIDE)

    def at(xx, yy, cc):
        return {"sector": ((yy % SIDE) * SIDE + xx % SIDE) * 2 + cc}

    def along(m, dmaj, dmin):
        return at(x + dmin, y + dmaj, c) if m == 0 else at(x + dmaj, y + dmin, c)

    major, minor = (y, x), (x, y)
    partner = at(x, y, 1 - c)
    up, down = {"row": (z + 1) % NZ}, {"row": (z + NZ - 1) % NZ}

    def slot(m, maj, mino):
        return 32 * m + ((maj % SIDE) * 2 + c) * SIDE + mino % SIDE

    barrier = pltpu.get_barrier_semaphore()
    partners = [along(0, 0, 1), along(0, 0, 3), along(0, 1, 0), along(0, 3, 0), partner, up, down]
    for device in partners:
        pl.semaphore_signal(barrier, inc=1, device_id=device, device_id_type=MESH)
    env_copy = pltpu.make_async_copy(env_ref, env_v, env_sem)
    env_copy.start()
    next_copy = pltpu.make_async_copy(next_hbm, next_ref, next_sem)
    next_copy.start()
    mine = [2 * sector, 2 * sector + 1]

    def find(n, found):
        return tuple(jnp.where(owner_ref[n] == slot_, n, f) for f, slot_ in zip(found, mine))

    sectors = lax.fori_loop(0, 64, find, (jnp.int32(0), jnp.int32(0)))
    limits, fields, source = [], [], []
    for t in range(2):
        limits.append(sizes_ref[sectors[t]] - z * ROWS)
        fields.append(charges_ref[sectors[t]].astype(jnp.float32) * (2.0 / 64))
        root_ref[t] = jnp.sqrt(jnp.full((8, T), sizes_ref[sectors[t]], jnp.int32).astype(jnp.float32))
        for n in range(4):
            place = owner_ref[pairs_ref[4 * sectors[t] + n]]
            px, py, pc = (place // 4) % SIDE, place // (4 * SIDE), (place // 2) % 2
            even = (py * 2 + pc) * SIDE + px
            odd = 32 + (px * 2 + pc) * SIDE + py
            source.append(jnp.where(place % 2 == 0, even, odd))
    row_ids = lax.broadcasted_iota(jnp.int32, (ROWS, T), 0)
    for j in range(CHUNKS):
        for m in range(2):
            value = block_ref[m, :, T * j : T * j + T].astype(jnp.float32)
            site_ref[j, m] = jnp.where(row_ids < limits[m], value, 0.0).astype(jnp.bfloat16)
    own = []
    for j in range(CHUNKS):
        for m in range(2):
            own.append(
                pltpu.make_async_copy(
                    site_ref.at[j, m], gath[j].at[slot(m, major[m], minor[m])], own_sem.at[j, m]
                )
            )
            own[-1].start()
    pl.semaphore_wait(barrier, len(partners))

    copies = {}

    def send(key, src, dst, ssem, rsem, device, late=False):
        copy = pltpu.make_async_remote_copy(
            src_ref=src, dst_ref=dst, send_sem=ssem, recv_sem=rsem, device_id=device, device_id_type=MESH
        )
        copies[key] = copy
        if not late:
            copy.start()

    def ag_send_one(j, m, n, ref, device, src=None):
        send((j, m, n), ref if src is None else src, ref, ag_send.at[j, m, n], ag_recv.at[j, m, n], device)

    def a1(j):
        for m in range(2):
            ref = gath[j].at[slot(m, major[m], minor[m])]
            ag_send_one(j, m, 0, ref, along(m, 0, 1), site_ref.at[j, m])
            ag_send_one(j, m, 1, ref, along(m, 0, 3), site_ref.at[j, m])

    def a2(j):
        for m in range(2):
            copies[j, m, 0].wait_recv()
            low = gath[j].at[slot(m, major[m], minor[m] + 3), pl.ds(0, ROWS // 2)]
            ag_send_one(j, m, 2, low, along(m, 0, 1))
            copies[j, m, 1].wait_recv()
            high = gath[j].at[slot(m, major[m], minor[m] + 1), pl.ds(ROWS // 2, ROWS // 2)]
            ag_send_one(j, m, 3, high, along(m, 0, 3))

    def group(j, m, dmaj, start=0, size=SIDE):
        return gath[j].at[pl.ds(slot(m, major[m] + dmaj, 0) + start, size)]

    def b1(j):
        for m in range(2):
            own[2 * j + m].wait()
            copies[j, m, 2].wait_recv()
            copies[j, m, 3].wait_recv()
            ag_send_one(j, m, 4, group(j, m, 0, 0, 2), along(m, 1, 0))
            ag_send_one(j, m, 5, group(j, m, 0, 2, 2), along(m, 3, 0))
            ag_send_one(j, m, 12, group(j, m, 0, 2, 2), along(m, 1, 0))
            ag_send_one(j, m, 13, group(j, m, 0, 0, 2), along(m, 3, 0))
            ag_send_one(j, m, 8, group(j, m, 0), partner)

    def b2(j):
        for m in range(2):
            copies[j, m, 4].wait_recv()
            ag_send_one(j, m, 6, group(j, m, 3, 0, 2), along(m, 1, 0))
            copies[j, m, 5].wait_recv()
            ag_send_one(j, m, 7, group(j, m, 1, 2, 2), along(m, 3, 0))

    def b2c(j):
        for m in range(2):
            copies[j, m, 12].wait_recv()
            copies[j, m, 13].wait_recv()
            ag_send_one(j, m, 9, group(j, m, 3), partner)
            ag_send_one(j, m, 10, group(j, m, 1), partner)

    def b3(j):
        for m in range(2):
            copies[j, m, 6].wait_recv()
            copies[j, m, 7].wait_recv()
            ag_send_one(j, m, 11, group(j, m, 2), partner)

    def ready(j):
        for m in range(2):
            for n in (8, 9, 10, 11):
                copies[j, m, n].wait_recv()
        if j == 0:
            env_copy.wait()

    def multiply(j, r):
        def one(n, carry):
            t = n % 2
            o = (n // 2) * (NZ - 2 * r) + r
            first = pl.multiple_of(((z + o) % NZ) * ROWS, ROWS)
            total = None
            for k in range(4):
                term = jnp.dot(
                    env_v[t, k, pl.ds(first, ROWS), :],
                    gath[j][jnp.where(t == 0, source[k], source[4 + k])],
                    preferred_element_type=jnp.float32,
                )
                total = term if total is None else total + term
            part[j, o, t] = total
            return carry

        lax.fori_loop(0, 2 if r in (0, 4) else 4, one, 0)

    def hop(j, s, direction, t):
        o = 5 - s if direction == 0 else 3 + s
        value = part[j, o, t]
        if s > first_hop(direction, t):
            copies["r", j, s - 1, direction, t].wait_recv()
            value = value + recv_b[j, direction, t, s - 2].astype(jnp.float32)
        send_b[j, direction, t, s - 1] = value.astype(jnp.bfloat16)
        send(
            ("r", j, s, direction, t),
            send_b.at[j, direction, t, s - 1],
            recv_b.at[j, direction, t, s - 1],
            rs_send.at[j, direction, t, s - 1],
            rs_recv.at[j, direction, t, s - 1],
            up if direction == 0 else down,
        )

    def finish(j, t):
        copies["r", j, 4, 0, t].wait_recv()
        copies["r", j, 4, 1, t].wait_recv()
        cols = pl.ds(T * j, T)
        total = part[j, 0, t] + fields[t] * site_ref[j, t].astype(jnp.float32)
        total = total + recv_b[j, 0, t, 3].astype(jnp.float32) + recv_b[j, 1, t, 3].astype(jnp.float32)
        bond_ref[t, :, cols] = jnp.where(row_ids < limits[t], total, 0.0)

    def grams(j):
        for t in range(2):
            for i in range(j + 1):
                value = dot(bond_ref[t, :, T * i : T * i + T], bond_ref[t, :, T * j : T * j + T], ((0,), (0,)))
                for q in range(NZ):
                    gp[j, q, t, i] = value[16 * q : 16 * q + 16]

    for j in range(CHUNKS):
        for s in range(1, 5):
            for direction, t in FLOWS:
                device = up if direction == 0 else down
                if s >= first_hop(direction, t):
                    send(
                        ("g", j, s, direction, t),
                        gsend.at[j, direction, t, s - 1, pl.ds(0, j + 1)],
                        grecv.at[j, direction, t, s - 1, pl.ds(0, j + 1)],
                        gr_send.at[j, direction, t, s - 1],
                        gr_recv.at[j, direction, t, s - 1],
                        device, late=True,
                    )
                if s < 4 or direction == t:
                    q = (z + NZ - (s - 1)) % NZ if direction == 0 else (z + s - 1) % NZ
                    piece = gfull.at[q, t, pl.ds(j * (j + 1) // 2, j + 1)]
                    send(
                        ("f", j, s, direction, t), piece, piece,
                        gg_send.at[j, direction, t, s - 1], gg_recv.at[j, direction, t, s - 1],
                        device, late=True,
                    )

    def gram_hop(j, s, direction, t):
        o = 5 - s if direction == 0 else 3 + s
        value = gp[j, (z + o) % NZ, t, : j + 1]
        if s > first_hop(direction, t):
            copies["g", j, s - 1, direction, t].wait_recv()
            value = value + grecv[j, direction, t, s - 2, : j + 1]
        gsend[j, direction, t, s - 1, : j + 1] = value
        copies["g", j, s, direction, t].start()

    def gram_sum(j, t):
        copies["g", j, 4, 0, t].wait_recv()
        copies["g", j, 4, 1, t].wait_recv()
        total = gp[j, z, t, : j + 1] + grecv[j, 0, t, 3, : j + 1] + grecv[j, 1, t, 3, : j + 1]
        gfull[z, t, j * (j + 1) // 2 : (j + 1) * (j + 2) // 2] = total

    def gram_round(j, s, direction, t):
        if s > 1:
            copies["f", j, s - 1, direction, t].wait_recv()
        copies["f", j, s, direction, t].start()

    def hops(j, s):
        for direction, t in FLOWS:
            if s >= first_hop(direction, t):
                gram_hop(j, s, direction, t)

    def sums(j):
        for t in range(2):
            gram_sum(j, t)

    def rounds(j, s):
        for direction, t in FLOWS:
            if s < 4 or direction == t:
                gram_round(j, s, direction, t)

    def last(j):
        for direction, t in FLOWS:
            copies["f", j, 4 if direction == t else 3, direction, t].wait_recv()
        for i in range(j + 1):
            for m in range(2):
                for q in range(NZ):
                    s_ref[m, i, j, 16 * q : 16 * q + 16, :] = gfull[q, m, j * (j + 1) // 2 + i]

    late_steps = {
        (0, 0): lambda: (last(0), hops(3, 1), sums(2), rounds(2, 1)),
        (0, 1): lambda: (hops(3, 2), rounds(2, 2)),
        (0, 2): lambda: (hops(3, 3), rounds(2, 3)),
        (1, 0): lambda: (last(1), hops(3, 4), rounds(2, 4)),
        (1, 1): lambda: (sums(3), rounds(3, 1)),
        (1, 2): lambda: rounds(3, 2),
        (2, 0): lambda: (last(2), rounds(3, 3)),
        (2, 1): lambda: rounds(3, 4),
        (3, 0): lambda: last(3),
    }

    def point(p, n):
        for (block, place), run in late_steps.items():
            if place == n:

                @pl.when(p == block)
                def _(run=run):
                    run()

    tasks = []

    def task(name, emit, time, needs=(), after=(), sends=()):
        tasks.append(dict(name=name, emit=emit, time=time, needs=needs, after=after, sends=sends))

    def axes(m):
        return ("x", "y") if m == 0 else ("y", "x")

    for j in range(CHUNKS):
        ms = range(2)
        mins, majs = [axes(m)[0] for m in ms], [axes(m)[1] for m in ms]
        task(("a1", j), lambda j=j: a1(j), 0.1,
             after=[[], [("a1", 0)], [("a2", 0)], [("b1", 1)]][j],
             sends=[((j, m, n), mins[m] + str(n), 64) for m in ms for n in (0, 1)])
        task(("a2", j), lambda j=j: a2(j), 0.1, needs=[(j, m, n) for m in ms for n in (0, 1)],
             sends=[((j, m, n + 2), mins[m] + str(n), 32) for m in ms for n in (0, 1)])
        task(("b1", j), lambda j=j: b1(j), 0.1, needs=[(j, m, n) for m in ms for n in (2, 3)],
             after=[("b2", j - 1)] if j else [],
             sends=[((j, m, n + 4 + late), majs[m] + str(n), 128) for m in ms for late in (0, 8) for n in (0, 1)]
             + [((j, m, 8), "c", 256) for m in ms])
        task(("b2", j), lambda j=j: b2(j), 0.1, needs=[(j, m, n) for m in ms for n in (4, 5)],
             sends=[((j, m, n + 6), majs[m] + str(n), 128) for m in ms for n in (0, 1)])
        task(("b2c", j), lambda j=j: b2c(j), 0.1, needs=[(j, m, n) for m in ms for n in (12, 13)],
             after=[("b2", j)], sends=[((j, m, n), "c", 256) for m in ms for n in (9, 10)])
        task(("b3", j), lambda j=j: b3(j), 0.1, needs=[(j, m, n) for m in ms for n in (6, 7)], after=[("b2c", j)],
             sends=[((j, m, 11), "c", 256) for m in ms])
        task(("ready", j), lambda j=j: ready(j), 0.1, needs=[(j, m, n) for m in ms for n in (8, 9, 10, 11)])
        before = ("ready", j)
        for r in (4, 3, 2, 1, 0):
            task(("mm", j, r), lambda j=j, r=r: multiply(j, r), 0.4 if r in (0, 4) else 0.8, after=[before])
            before = ("mm", j, r)
            if r == 0:
                continue
            s = 5 - r
            for direction, t in FLOWS:
                if s >= first_hop(direction, t):
                    more = s > first_hop(direction, t)
                    task(("hop", j, s, direction, t),
                         lambda j=j, s=s, direction=direction, t=t: hop(j, s, direction, t), 0.1,
                         needs=[("r", j, s - 1, direction, t)] if more else [], after=[before],
                         sends=[(("r", j, s, direction, t), "z" + str(direction), 64)])
        for t in range(2):
            task(("finish", j, t), lambda j=j, t=t: finish(j, t), 0.1,
                 needs=[("r", j, 4, 0, t), ("r", j, 4, 1, t)], after=[("mm", j, 0)])
        task(("gram", j), lambda j=j: grams(j), 0.4 + 0.4 * j,
             after=[("finish", j, 0), ("finish", j, 1)] + ([("gram", j - 1)] if j else []))
        for s in range(1, 5):
            for direction, t in FLOWS:
                if s >= first_hop(direction, t) and j < 3:
                    more = s > first_hop(direction, t)
                    task(("ghop", j, s, direction, t),
                         lambda j=j, s=s, direction=direction, t=t: gram_hop(j, s, direction, t), 0.1,
                         needs=[("g", j, s - 1, direction, t)] if more else [], after=[("gram", j)],
                         sends=[(("g", j, s, direction, t), "z" + str(direction), 8 * (j + 1))])
        for t in range(2 if j < 2 else 0):
            task(("gsum", j, t), lambda j=j, t=t: gram_sum(j, t), 0.1,
                 needs=[("g", j, 4, 0, t), ("g", j, 4, 1, t)], after=[("gram", j)])
        for s in range(1, 5):
            for direction, t in FLOWS:
                if j < 2 and (s < 4 or direction == t):
                    task(("ground", j, s, direction, t),
                         lambda j=j, s=s, direction=direction, t=t: gram_round(j, s, direction, t), 0.1,
                         needs=[("f", j, s - 1, direction, t)] if s > 1 else [], after=[("gsum", j, t)],
                         sends=[(("f", j, s, direction, t), "z" + str(direction), 8 * (j + 1))])
    for item in ordered(tasks):
        item["emit"]()

    def block(p, carry):
        point(p, 0)
        def column(i, c):
            def above(k, c2):
                for m in range(2):
                    s_ref[m, i, p] = s_ref[m, i, p] - dot(s_ref[m, k, i], s_ref[m, k, p], ((0,), (0,)))
                return c2

            lax.fori_loop(0, i, above, 0)
            for m in range(2):
                value = dot(d_ref[m, i], s_ref[m, i, p], ((1,), (0,)))
                s_ref[m, i, p] = value
                s_ref[m, p, p] = s_ref[m, p, p] - dot(value, value, ((0,), (0,)))
            return c

        lax.fori_loop(0, p, column, 0)
        factor_block([s_ref[m, p, p] for m in range(2)], u_ref, w_ref, r_ref, lambda: point(p, 1))
        for m in range(2):
            d_ref[m, p] = w_ref[m]
            s_ref[m, p, p] = u_ref[m]
        point(p, 2)
        return carry

    lax.fori_loop(0, NB, block, 0)
    next_copy.wait()
    row16 = lax.broadcasted_iota(jnp.int32, (16, T), 0)
    lane16 = lax.broadcasted_iota(jnp.int32, (16, T), 1)
    for m in range(2):
        trace = jnp.zeros((16, T), jnp.float32)
        for p in range(NB):
            for q in range(NZ):
                trace = trace + jnp.where(lane16 == row16 + 16 * q, gfull[q, m, p * (p + 3) // 2], 0.0)
        scale = lax.rsqrt(jnp.full((1, T), jnp.sum(trace) / (NB * T) + 1e-6, jnp.float32))
        solved = []
        for j in range(NB):
            value = bond_ref[m, :, T * j : T * j + T]
            for i in range(j):
                value = value - dot(solved[i], s_ref[m, i, j], ((1,), (0,)))
            value = dot(value, d_ref[m, j], ((1,), (1,)))
            solved.append(value)
            iso_ref[m, :, T * j : T * j + T] = value * root_ref[m, :1, :]
        for p in range(NB):
            total = None
            for i in range(p, NB):
                up_block = (s_ref[m, p, i] * scale).astype(jnp.bfloat16)
                term = dot(up_block, next_ref[m, T * i : T * i + T, :], ((1,), (0,)), None)
                total = term if total is None else total + term
            adv_ref[m, T * p : T * p + T, :] = total.astype(jnp.bfloat16)
    for copy in copies.values():
        copy.wait_send()


def site_step(owner, pairs, sizes, charges, environment, site_block, next_site):
    vmem, anywhere = pl.BlockSpec(memory_space=pltpu.VMEM), pl.BlockSpec(memory_space=pl.ANY)
    bf, f32 = jnp.bfloat16, jnp.float32
    dma = pltpu.SemaphoreType.DMA
    blocks = NB * (NB + 1) // 2
    return pl.pallas_call(
        bond_kernel,
        out_shape=(
            jax.ShapeDtypeStruct(site_block.shape, f32),
            jax.ShapeDtypeStruct(next_site.shape, bf),
        ),
        in_specs=[pl.BlockSpec(memory_space=pltpu.SMEM)] * 4 + [anywhere, vmem, anywhere],
        out_specs=(vmem, vmem),
        scratch_shapes=[pltpu.VMEM((64, ROWS, T), bf)] * CHUNKS
        + [
            pltpu.VMEM((CHUNKS, 2, ROWS, T), bf),
            pltpu.VMEM(environment.shape, bf),
            pltpu.VMEM((CHUNKS, NZ, 2, ROWS, T), f32),
            pltpu.VMEM((CHUNKS, 2, 2, 4, ROWS, T), bf),
            pltpu.VMEM((CHUNKS, 2, 2, 4, ROWS, T), bf),
            pltpu.VMEM((CHUNKS, NZ, 2, NB, 16, T), f32),
            pltpu.VMEM((CHUNKS, 2, 2, 4, NB, 16, T), f32),
            pltpu.VMEM((CHUNKS, 2, 2, 4, NB, 16, T), f32),
            pltpu.VMEM((NZ, 2, blocks, 16, T), f32),
            pltpu.VMEM(site_block.shape, f32),
            pltpu.VMEM((2, 8, T), f32),
            pltpu.VMEM(next_site.shape, bf),
            pltpu.VMEM((2, NB, NB, T, T), f32),
            pltpu.VMEM((2, NB, T, T), f32),
            pltpu.VMEM((2, T, T), f32),
            pltpu.VMEM((2, T, T), f32),
            pltpu.VMEM((2, HALF, T), f32),
            dma,
            dma,
            dma((CHUNKS, 2)),
            dma((CHUNKS, 2, 14)),
            dma((CHUNKS, 2, 14)),
            dma((CHUNKS, 2, 2, 4)),
            dma((CHUNKS, 2, 2, 4)),
            dma((CHUNKS, 2, 2, 4)),
            dma((CHUNKS, 2, 2, 4)),
            dma((CHUNKS, 2, 2, 4)),
            dma((CHUNKS, 2, 2, 4)),
        ],
        compiler_params=pltpu.CompilerParams(
            vmem_limit_bytes=63 * 1024 * 1024, collective_id=0, has_side_effects=True
        ),
        name="bond",
    )(owner, pairs, sizes, charges, environment, site_block, next_site)


def local(environment, site_block, next_site, charges, sizes, pairs, owner):
    iso, advanced = site_step(
        owner, pairs.reshape(-1), sizes, charges, environment, site_block, next_site
    )
    return (jnp.swapaxes(iso, 0, 1), advanced)


def solution(mesh):
    return jax.shard_map(
        local,
        mesh=mesh,
        in_specs=(
            P("sector", None, None, "row"),
            P("sector", "row", None),
            P("sector", None, "row"),
            P(),
            P(),
            P(),
            P(),
        ),
        out_specs=(P("row", "sector", None), P("sector", None, "row")),
        check_vma=False,
    )
```

```python
import jax
import jax.numpy as jnp
from jax import lax
from jax.experimental import pallas as pl
from jax.experimental.pallas import tpu as pltpu
from jax.sharding import PartitionSpec as P

NB = 4
T = 128
GROUP = 8
HALF = 64
HI = lax.Precision.HIGHEST


def dot(a, b, dims, precision=HI):
    return lax.dot_general(
        a, b, (dims, ((), ())), precision=precision, preferred_element_type=jnp.float32
    )


def factor_tiles(a_tiles, r_ref, inside=None):
    count = len(a_tiles)
    rows8 = HALF // 8
    lane = lax.broadcasted_iota(jnp.int32, (8, T), 1)
    sub = lax.broadcasted_iota(jnp.int32, (8, T), 0)

    def spread(x, s):
        return jnp.broadcast_to(x[s : s + 1, :], (8, T))

    for j0 in range(0, HALF, GROUP):
        if inside is not None and j0 == 6 * GROUP:
            inside()
        g = j0 // 8
        s0 = j0 - 8 * g
        state = []
        for m in range(count):
            cols = [
                [
                    jnp.broadcast_to(a_tiles[m][i][:, j0 + k : j0 + k + 1], (8, T))
                    for i in range(g, rows8)
                ]
                for k in range(GROUP)
            ]
            rows = [spread(a_tiles[m][g], s0 + k) for k in range(GROUP)]
            state.append((cols, rows))
        for k in range(GROUP):
            for m in range(count):
                cols, rows = state[m]
                rs = lax.rsqrt(spread(cols[k][0], s0 + k))
                cols[k] = [c * rs for c in cols[k]]
                rows[k] = rows[k] * rs
                for q in range(k + 1, GROUP):
                    f = spread(cols[k][0], s0 + q)
                    cols[q] = [c - l * f for c, l in zip(cols[q], cols[k])]
                    rows[q] = rows[q] - rows[k] * f
        for m in range(count):
            cols, rows = state[m]
            for k in range(GROUP):
                j = j0 + k
                r_ref[m, j : j + 1, :] = jnp.where(lane[:1] >= j, rows[k][:1], 0.0)
            last = s0 + GROUP == 8
            for i in range(g + 1 if last else g, rows8):
                a = a_tiles[m][i]
                for k in range(GROUP):
                    l = cols[k][i - g]
                    if i == g:
                        l = jnp.where(sub >= s0 + GROUP, l, 0.0)
                    a = a - l * rows[k]
                a_tiles[m][i] = a


def factor_block(a_list, u_ref, w_ref, r_ref, between, inside):
    lane = lax.broadcasted_iota(jnp.int32, (HALF, T), 1)
    row = lax.broadcasted_iota(jnp.int32, (HALF, T), 0)
    first = lane < HALF
    eye = jnp.where(lane == row + HALF, 1.0, 0.0).astype(jnp.float32)

    def turn(v):
        return pltpu.roll(v, HALF, 1)

    def tiles(v):
        return [v[8 * i : 8 * i + 8] for i in range(HALF // 8)]

    factor_tiles([tiles(jnp.where(first, a[:HALF], eye)) for a in a_list], r_ref)
    kept, second = [], []
    for m, a in enumerate(a_list):
        r1 = r_ref[m]
        w1 = turn(r1)
        top = dot(w1[:, :HALF], a[:HALF], ((1,), (0,)))
        rest = a[HALF:] - dot(top[:, HALF:], top, ((0,), (0,)))
        kept.append((jnp.where(first, w1, 0.0), top))
        second.append(tiles(jnp.where(first, turn(rest), eye)))
        u_ref[m, :HALF] = jnp.where(first, r1, top)
        w_ref[m, :HALF] = jnp.where(first, w1, 0.0)
    between()
    factor_tiles(second, r_ref, inside)
    for m, (w1, top) in enumerate(kept):
        r2 = r_ref[m]
        w2 = turn(r2)
        u_ref[m, HALF:] = jnp.where(first, 0.0, w2)
        low = dot(top[:, HALF:], w1, ((0,), (0,)))
        w_ref[m, HALF:] = jnp.where(first, -dot(w2[:, :HALF], low, ((1,), (0,))), r2)


CHUNKS = 4
NZ = 8
SIDE = 4
ROWS = 256
MESH = pl.DeviceIdType.MESH
FLOWS = [(0, 0), (1, 1), (0, 1), (1, 0)]


def first_hop(direction, t):
    return 1 if direction == t else 2


def ordered(tasks):
    rate = {"x": 43.0, "y": 43.0, "z": 43.0, "c": 300.0}
    link_free, arrival, done, order = {}, {}, set(), []
    now, left = 0.0, list(tasks)
    while left:
        best = None
        for n, task in enumerate(left):
            if all(a in done for a in task["after"]) and all(k in arrival for k in task["needs"]):
                start = max([now] + [arrival[k] for k in task["needs"]])
                if best is None or start < best[0]:
                    best = (start, n)
        start, n = best
        task = left.pop(n)
        now = start + task["time"]
        for key, link, kib in task["sends"]:
            begin = max(now, link_free.get(link, 0.0))
            link_free[link] = begin + kib / rate[link[0]]
            arrival[key] = link_free[link] + (1.0 if link[0] == "c" else 1.8)
        done.add(task["name"])
        order.append(task)
    return order


def bond_kernel(
    owner_ref, pairs_ref, sizes_ref, charges_ref, env_ref, block_ref, next_hbm, iso_ref, adv_ref,
    g0, g1, g2, g3, site_ref, env_v, part, send_b, recv_b, gp, gsend, grecv, gfull,
    bond_ref, root_ref, next_ref, s_ref, d_ref, u_ref, w_ref, r_ref,
    env_sem, next_sem, own_sem, ag_send, ag_recv, rs_send, rs_recv, gr_send, gr_recv, gg_send, gg_recv,
):
    gath = (g0, g1, g2, g3)
    sector, z = lax.axis_index("sector"), lax.axis_index("row")
    c = sector % 2
    x = (sector // 2) % SIDE
    y = sector // (2 * SIDE)

    def at(xx, yy, cc):
        return {"sector": ((yy % SIDE) * SIDE + xx % SIDE) * 2 + cc}

    def along(m, dmaj, dmin):
        return at(x + dmin, y + dmaj, c) if m == 0 else at(x + dmaj, y + dmin, c)

    major, minor = (y, x), (x, y)
    partner = at(x, y, 1 - c)
    up, down = {"row": (z + 1) % NZ}, {"row": (z + NZ - 1) % NZ}

    def slot(m, maj, mino):
        return 32 * m + ((maj % SIDE) * 2 + c) * SIDE + mino % SIDE

    barrier = pltpu.get_barrier_semaphore()
    partners = [along(0, 0, 1), along(0, 0, 3), along(0, 1, 0), along(0, 3, 0), partner, up, down]
    for device in partners:
        pl.semaphore_signal(barrier, inc=1, device_id=device, device_id_type=MESH)
    env_copy = pltpu.make_async_copy(env_ref, env_v, env_sem)
    env_copy.start()
    next_copy = pltpu.make_async_copy(next_hbm, next_ref, next_sem)
    next_copy.start()
    mine = [2 * sector, 2 * sector + 1]

    def find(n, found):
        return tuple(jnp.where(owner_ref[n] == slot_, n, f) for f, slot_ in zip(found, mine))

    sectors = lax.fori_loop(0, 64, find, (jnp.int32(0), jnp.int32(0)))
    limits, fields, source = [], [], []
    for t in range(2):
        limits.append(sizes_ref[sectors[t]] - z * ROWS)
        fields.append(charges_ref[sectors[t]].astype(jnp.float32) * (2.0 / 64))
        root_ref[t] = jnp.sqrt(jnp.full((8, T), sizes_ref[sectors[t]], jnp.int32).astype(jnp.float32))
        for n in range(4):
            place = owner_ref[pairs_ref[4 * sectors[t] + n]]
            px, py, pc = (place // 4) % SIDE, place // (4 * SIDE), (place // 2) % 2
            even = (py * 2 + pc) * SIDE + px
            odd = 32 + (px * 2 + pc) * SIDE + py
            source.append(jnp.where(place % 2 == 0, even, odd))
    row_ids = lax.broadcasted_iota(jnp.int32, (ROWS, T), 0)
    for j in range(CHUNKS):
        for m in range(2):
            value = block_ref[m, :, T * j : T * j + T].astype(jnp.float32)
            site_ref[j, m] = jnp.where(row_ids < limits[m], value, 0.0).astype(jnp.bfloat16)
    own = []
    for j in range(CHUNKS):
        for m in range(2):
            own.append(
                pltpu.make_async_copy(
                    site_ref.at[j, m], gath[j].at[slot(m, major[m], minor[m])], own_sem.at[j, m]
                )
            )
            own[-1].start()
    pl.semaphore_wait(barrier, len(partners))

    copies = {}

    def send(key, src, dst, ssem, rsem, device, late=False):
        copy = pltpu.make_async_remote_copy(
            src_ref=src, dst_ref=dst, send_sem=ssem, recv_sem=rsem, device_id=device, device_id_type=MESH
        )
        copies[key] = copy
        if not late:
            copy.start()

    def ag_send_one(j, m, n, ref, device, src=None):
        send((j, m, n), ref if src is None else src, ref, ag_send.at[j, m, n], ag_recv.at[j, m, n], device)

    def a1(j):
        for m in range(2):
            ref = gath[j].at[slot(m, major[m], minor[m])]
            ag_send_one(j, m, 0, ref, along(m, 0, 1), site_ref.at[j, m])
            ag_send_one(j, m, 1, ref, along(m, 0, 3), site_ref.at[j, m])

    def a2(j):
        for m in range(2):
            copies[j, m, 0].wait_recv()
            low = gath[j].at[slot(m, major[m], minor[m] + 3), pl.ds(0, ROWS // 2)]
            ag_send_one(j, m, 2, low, along(m, 0, 1))
            copies[j, m, 1].wait_recv()
            high = gath[j].at[slot(m, major[m], minor[m] + 1), pl.ds(ROWS // 2, ROWS // 2)]
            ag_send_one(j, m, 3, high, along(m, 0, 3))

    def group(j, m, dmaj, start=0, size=SIDE):
        return gath[j].at[pl.ds(slot(m, major[m] + dmaj, 0) + start, size)]

    def b1(j):
        for m in range(2):
            own[2 * j + m].wait()
            copies[j, m, 2].wait_recv()
            copies[j, m, 3].wait_recv()
            ag_send_one(j, m, 4, group(j, m, 0, 0, 2), along(m, 1, 0))
            ag_send_one(j, m, 5, group(j, m, 0, 2, 2), along(m, 3, 0))
            ag_send_one(j, m, 12, group(j, m, 0, 2, 2), along(m, 1, 0))
            ag_send_one(j, m, 13, group(j, m, 0, 0, 2), along(m, 3, 0))
            ag_send_one(j, m, 8, group(j, m, 0), partner)

    def b2(j):
        for m in range(2):
            copies[j, m, 4].wait_recv()
            ag_send_one(j, m, 6, group(j, m, 3, 0, 2), along(m, 1, 0))
            copies[j, m, 5].wait_recv()
            ag_send_one(j, m, 7, group(j, m, 1, 2, 2), along(m, 3, 0))

    def b2c(j):
        for m in range(2):
            copies[j, m, 12].wait_recv()
            copies[j, m, 13].wait_recv()
            ag_send_one(j, m, 9, group(j, m, 3), partner)
            ag_send_one(j, m, 10, group(j, m, 1), partner)

    def b3(j):
        for m in range(2):
            copies[j, m, 6].wait_recv()
            copies[j, m, 7].wait_recv()
            ag_send_one(j, m, 11, group(j, m, 2), partner)

    def ready(j):
        for m in range(2):
            for n in (8, 9, 10, 11):
                copies[j, m, n].wait_recv()
        if j == 0:
            env_copy.wait()

    def multiply(j, r):
        def one(n, carry):
            t = n % 2
            o = (n // 2) * (NZ - 2 * r) + r
            first = pl.multiple_of(((z + o) % NZ) * ROWS, ROWS)
            total = None
            for k in range(4):
                term = jnp.dot(
                    env_v[t, k, pl.ds(first, ROWS), :],
                    gath[j][jnp.where(t == 0, source[k], source[4 + k])],
                    preferred_element_type=jnp.float32,
                )
                total = term if total is None else total + term
            part[j, o, t] = total
            return carry

        lax.fori_loop(0, 2 if r in (0, 4) else 4, one, 0)

    def hop(j, s, direction, t):
        o = 5 - s if direction == 0 else 3 + s
        value = part[j, o, t]
        if s > first_hop(direction, t):
            copies["r", j, s - 1, direction, t].wait_recv()
            value = value + recv_b[j, direction, t, s - 2].astype(jnp.float32)
        send_b[j, direction, t, s - 1] = value.astype(jnp.bfloat16)
        send(
            ("r", j, s, direction, t),
            send_b.at[j, direction, t, s - 1],
            recv_b.at[j, direction, t, s - 1],
            rs_send.at[j, direction, t, s - 1],
            rs_recv.at[j, direction, t, s - 1],
            up if direction == 0 else down,
        )

    def finish(j, t):
        copies["r", j, 4, 0, t].wait_recv()
        copies["r", j, 4, 1, t].wait_recv()
        cols = pl.ds(T * j, T)
        total = part[j, 0, t] + fields[t] * site_ref[j, t].astype(jnp.float32)
        total = total + recv_b[j, 0, t, 3].astype(jnp.float32) + recv_b[j, 1, t, 3].astype(jnp.float32)
        bond_ref[t, :, cols] = jnp.where(row_ids < limits[t], total, 0.0)

    def grams(j):
        for t in range(2):
            for i in range(j + 1):
                value = dot(bond_ref[t, :, T * i : T * i + T], bond_ref[t, :, T * j : T * j + T], ((0,), (0,)))
                for q in range(NZ):
                    gp[j, q, t, i] = value[16 * q : 16 * q + 16]

    for j in range(CHUNKS):
        for s in range(1, 5):
            for direction, t in FLOWS:
                device = up if direction == 0 else down
                if s >= first_hop(direction, t):
                    send(
                        ("g", j, s, direction, t),
                        gsend.at[j, direction, t, s - 1, pl.ds(0, j + 1)],
                        grecv.at[j, direction, t, s - 1, pl.ds(0, j + 1)],
                        gr_send.at[j, direction, t, s - 1],
                        gr_recv.at[j, direction, t, s - 1],
                        device, late=True,
                    )
                if s < 4 or direction == t:
                    q = (z + NZ - (s - 1)) % NZ if direction == 0 else (z + s - 1) % NZ
                    piece = gfull.at[q, t, pl.ds(j * (j + 1) // 2, j + 1)]
                    send(
                        ("f", j, s, direction, t), piece, piece,
                        gg_send.at[j, direction, t, s - 1], gg_recv.at[j, direction, t, s - 1],
                        device, late=True,
                    )

    def gram_hop(j, s, direction, t):
        o = 5 - s if direction == 0 else 3 + s
        value = gp[j, (z + o) % NZ, t, : j + 1]
        if s > first_hop(direction, t):
            copies["g", j, s - 1, direction, t].wait_recv()
            value = value + grecv[j, direction, t, s - 2, : j + 1]
        gsend[j, direction, t, s - 1, : j + 1] = value
        copies["g", j, s, direction, t].start()

    def gram_sum(j, t):
        copies["g", j, 4, 0, t].wait_recv()
        copies["g", j, 4, 1, t].wait_recv()
        total = gp[j, z, t, : j + 1] + grecv[j, 0, t, 3, : j + 1] + grecv[j, 1, t, 3, : j + 1]
        gfull[z, t, j * (j + 1) // 2 : (j + 1) * (j + 2) // 2] = total

    def gram_round(j, s, direction, t):
        if s > 1:
            copies["f", j, s - 1, direction, t].wait_recv()
        copies["f", j, s, direction, t].start()

    def hops(j, s):
        for direction, t in FLOWS:
            if s >= first_hop(direction, t):
                gram_hop(j, s, direction, t)

    def sums(j):
        for t in range(2):
            gram_sum(j, t)

    def rounds(j, s):
        for direction, t in FLOWS:
            if s < 4 or direction == t:
                gram_round(j, s, direction, t)

    def last(j):
        for direction, t in FLOWS:
            copies["f", j, 4 if direction == t else 3, direction, t].wait_recv()
        for i in range(j + 1):
            for m in range(2):
                for q in range(NZ):
                    s_ref[m, i, j, 16 * q : 16 * q + 16, :] = gfull[q, m, j * (j + 1) // 2 + i]

    late_steps = {
        (0, 0): lambda: (last(0), hops(3, 1), sums(2), rounds(2, 1)),
        (0, 2): lambda: (hops(3, 2), rounds(2, 2)),
        (0, 3): lambda: (hops(3, 3), rounds(2, 3)),
        (1, 0): lambda: last(1),
        (1, 1): lambda: (hops(3, 4), rounds(2, 4)),
        (1, 2): lambda: (sums(3), rounds(3, 1)),
        (1, 3): lambda: rounds(3, 2),
        (2, 0): lambda: last(2),
        (2, 1): lambda: rounds(3, 3),
        (2, 2): lambda: rounds(3, 4),
        (3, 0): lambda: last(3),
    }

    def point(p, n):
        for (block, place), run in late_steps.items():
            if place == n:

                @pl.when(p == block)
                def _(run=run):
                    run()

    tasks = []

    def task(name, emit, time, needs=(), after=(), sends=()):
        tasks.append(dict(name=name, emit=emit, time=time, needs=needs, after=after, sends=sends))

    def axes(m):
        return ("x", "y") if m == 0 else ("y", "x")

    for j in range(CHUNKS):
        ms = range(2)
        mins, majs = [axes(m)[0] for m in ms], [axes(m)[1] for m in ms]
        task(("a1", j), lambda j=j: a1(j), 0.1,
             after=[[], [("a1", 0)], [("a2", 0)], [("b1", 1)]][j],
             sends=[((j, m, n), mins[m] + str(n), 64) for m in ms for n in (0, 1)])
        task(("a2", j), lambda j=j: a2(j), 0.1, needs=[(j, m, n) for m in ms for n in (0, 1)],
             sends=[((j, m, n + 2), mins[m] + str(n), 32) for m in ms for n in (0, 1)])
        task(("b1", j), lambda j=j: b1(j), 0.1, needs=[(j, m, n) for m in ms for n in (2, 3)],
             after=[("b2", j - 1)] if j else [],
             sends=[((j, m, n + 4 + late), majs[m] + str(n), 128) for m in ms for late in (0, 8) for n in (0, 1)]
             + [((j, m, 8), "c", 256) for m in ms])
        task(("b2", j), lambda j=j: b2(j), 0.1, needs=[(j, m, n) for m in ms for n in (4, 5)],
             sends=[((j, m, n + 6), majs[m] + str(n), 128) for m in ms for n in (0, 1)])
        task(("b2c", j), lambda j=j: b2c(j), 0.1, needs=[(j, m, n) for m in ms for n in (12, 13)],
             after=[("b2", j)], sends=[((j, m, n), "c", 256) for m in ms for n in (9, 10)])
        task(("b3", j), lambda j=j: b3(j), 0.1, needs=[(j, m, n) for m in ms for n in (6, 7)], after=[("b2c", j)],
             sends=[((j, m, 11), "c", 256) for m in ms])
        task(("ready", j), lambda j=j: ready(j), 0.1, needs=[(j, m, n) for m in ms for n in (8, 9, 10, 11)])
        before = ("ready", j)
        for r in (4, 3, 2, 1, 0):
            task(("mm", j, r), lambda j=j, r=r: multiply(j, r), 0.4 if r in (0, 4) else 0.8, after=[before])
            before = ("mm", j, r)
            if r == 0:
                continue
            s = 5 - r
            for direction, t in FLOWS:
                if s >= first_hop(direction, t):
                    more = s > first_hop(direction, t)
                    task(("hop", j, s, direction, t),
                         lambda j=j, s=s, direction=direction, t=t: hop(j, s, direction, t), 0.1,
                         needs=[("r", j, s - 1, direction, t)] if more else [], after=[before],
                         sends=[(("r", j, s, direction, t), "z" + str(direction), 64)])
        for t in range(2):
            task(("finish", j, t), lambda j=j, t=t: finish(j, t), 0.1,
                 needs=[("r", j, 4, 0, t), ("r", j, 4, 1, t)], after=[("mm", j, 0)])
        task(("gram", j), lambda j=j: grams(j), 0.4 + 0.4 * j,
             after=[("finish", j, 0), ("finish", j, 1)] + ([("gram", j - 1)] if j else []))
        for s in range(1, 5):
            for direction, t in FLOWS:
                if s >= first_hop(direction, t) and j < 3:
                    more = s > first_hop(direction, t)
                    task(("ghop", j, s, direction, t),
                         lambda j=j, s=s, direction=direction, t=t: gram_hop(j, s, direction, t), 0.1,
                         needs=[("g", j, s - 1, direction, t)] if more else [], after=[("gram", j)],
                         sends=[(("g", j, s, direction, t), "z" + str(direction), 8 * (j + 1))])
        for t in range(2 if j < 2 else 0):
            task(("gsum", j, t), lambda j=j, t=t: gram_sum(j, t), 0.1,
                 needs=[("g", j, 4, 0, t), ("g", j, 4, 1, t)], after=[("gram", j)])
        for s in range(1, 5):
            for direction, t in FLOWS:
                if j < 2 and (s < 4 or direction == t):
                    task(("ground", j, s, direction, t),
                         lambda j=j, s=s, direction=direction, t=t: gram_round(j, s, direction, t), 0.1,
                         needs=[("f", j, s - 1, direction, t)] if s > 1 else [], after=[("gsum", j, t)],
                         sends=[(("f", j, s, direction, t), "z" + str(direction), 8 * (j + 1))])
    for item in ordered(tasks):
        item["emit"]()

    def block(p, carry):
        point(p, 0)
        def column(i, c):
            def above(k, c2):
                for m in range(2):
                    s_ref[m, i, p] = s_ref[m, i, p] - dot(s_ref[m, k, i], s_ref[m, k, p], ((0,), (0,)))
                return c2

            lax.fori_loop(0, i, above, 0)
            for m in range(2):
                value = dot(d_ref[m, i], s_ref[m, i, p], ((1,), (0,)))
                s_ref[m, i, p] = value
                s_ref[m, p, p] = s_ref[m, p, p] - dot(value, value, ((0,), (0,)))
            return c

        lax.fori_loop(0, p, column, 0)
        point(p, 1)
        factor_block(
            [s_ref[m, p, p] for m in range(2)], u_ref, w_ref, r_ref,
            lambda: point(p, 2), lambda: point(p, 3),
        )
        for m in range(2):
            d_ref[m, p] = w_ref[m]
            s_ref[m, p, p] = u_ref[m]
        cols = pl.ds(pl.multiple_of(p * T, T), T)

        def left(i, c):
            before = pl.ds(pl.multiple_of(i * T, T), T)
            for m in range(2):
                term = dot(bond_ref[m, :, before], s_ref[m, i, p], ((1,), (0,)))
                bond_ref[m, :, cols] = bond_ref[m, :, cols] - term
            return c

        lax.fori_loop(0, p, left, 0)
        for m in range(2):
            value = dot(bond_ref[m, :, cols], d_ref[m, p], ((1,), (1,)))
            bond_ref[m, :, cols] = value
            iso_ref[m, :, cols] = value * root_ref[m, :1, :]
        return carry

    lax.fori_loop(0, NB, block, 0)
    next_copy.wait()
    row16 = lax.broadcasted_iota(jnp.int32, (16, T), 0)
    lane16 = lax.broadcasted_iota(jnp.int32, (16, T), 1)
    for m in range(2):
        trace = jnp.zeros((16, T), jnp.float32)
        for p in range(NB):
            for q in range(NZ):
                trace = trace + jnp.where(lane16 == row16 + 16 * q, gfull[q, m, p * (p + 3) // 2], 0.0)
        scale = lax.rsqrt(jnp.full((1, T), jnp.sum(trace) / (NB * T) + 1e-6, jnp.float32))
        for p in range(NB):
            total = None
            for i in range(p, NB):
                up_block = (s_ref[m, p, i] * scale).astype(jnp.bfloat16)
                term = dot(up_block, next_ref[m, T * i : T * i + T, :], ((1,), (0,)), None)
                total = term if total is None else total + term
            adv_ref[m, T * p : T * p + T, :] = total.astype(jnp.bfloat16)
    for copy in copies.values():
        copy.wait_send()


def site_step(owner, pairs, sizes, charges, environment, site_block, next_site):
    vmem, anywhere = pl.BlockSpec(memory_space=pltpu.VMEM), pl.BlockSpec(memory_space=pl.ANY)
    bf, f32 = jnp.bfloat16, jnp.float32
    dma = pltpu.SemaphoreType.DMA
    blocks = NB * (NB + 1) // 2
    return pl.pallas_call(
        bond_kernel,
        out_shape=(
            jax.ShapeDtypeStruct(site_block.shape, f32),
            jax.ShapeDtypeStruct(next_site.shape, bf),
        ),
        in_specs=[pl.BlockSpec(memory_space=pltpu.SMEM)] * 4 + [anywhere, vmem, anywhere],
        out_specs=(vmem, vmem),
        scratch_shapes=[pltpu.VMEM((64, ROWS, T), bf)] * CHUNKS
        + [
            pltpu.VMEM((CHUNKS, 2, ROWS, T), bf),
            pltpu.VMEM(environment.shape, bf),
            pltpu.VMEM((CHUNKS, NZ, 2, ROWS, T), f32),
            pltpu.VMEM((CHUNKS, 2, 2, 4, ROWS, T), bf),
            pltpu.VMEM((CHUNKS, 2, 2, 4, ROWS, T), bf),
            pltpu.VMEM((CHUNKS, NZ, 2, NB, 16, T), f32),
            pltpu.VMEM((CHUNKS, 2, 2, 4, NB, 16, T), f32),
            pltpu.VMEM((CHUNKS, 2, 2, 4, NB, 16, T), f32),
            pltpu.VMEM((NZ, 2, blocks, 16, T), f32),
            pltpu.VMEM(site_block.shape, f32),
            pltpu.VMEM((2, 8, T), f32),
            pltpu.VMEM(next_site.shape, bf),
            pltpu.VMEM((2, NB, NB, T, T), f32),
            pltpu.VMEM((2, NB, T, T), f32),
            pltpu.VMEM((2, T, T), f32),
            pltpu.VMEM((2, T, T), f32),
            pltpu.VMEM((2, HALF, T), f32),
            dma,
            dma,
            dma((CHUNKS, 2)),
            dma((CHUNKS, 2, 14)),
            dma((CHUNKS, 2, 14)),
            dma((CHUNKS, 2, 2, 4)),
            dma((CHUNKS, 2, 2, 4)),
            dma((CHUNKS, 2, 2, 4)),
            dma((CHUNKS, 2, 2, 4)),
            dma((CHUNKS, 2, 2, 4)),
            dma((CHUNKS, 2, 2, 4)),
        ],
        compiler_params=pltpu.CompilerParams(
            vmem_limit_bytes=63 * 1024 * 1024, collective_id=0, has_side_effects=True
        ),
        name="bond",
    )(owner, pairs, sizes, charges, environment, site_block, next_site)


def local(environment, site_block, next_site, charges, sizes, pairs, owner):
    iso, advanced = site_step(
        owner, pairs.reshape(-1), sizes, charges, environment, site_block, next_site
    )
    return (jnp.swapaxes(iso, 0, 1), advanced)


def solution(mesh):
    return jax.shard_map(
        local,
        mesh=mesh,
        in_specs=(
            P("sector", None, None, "row"),
            P("sector", "row", None),
            P("sector", None, "row"),
            P(),
            P(),
            P(),
            P(),
        ),
        out_specs=(P("row", "sector", None), P("sector", None, "row")),
        check_vma=False,
    )
```

```python
import jax
import jax.numpy as jnp
from jax import lax
from jax.experimental import pallas as pl
from jax.experimental.pallas import tpu as pltpu
from jax.sharding import PartitionSpec as P

NB = 4
T = 128
GROUP = 8
HALF = 64
HI = lax.Precision.HIGHEST


def dot(a, b, dims, precision=HI):
    return lax.dot_general(
        a, b, (dims, ((), ())), precision=precision, preferred_element_type=jnp.float32
    )


def factor_tiles(a_tiles, r_ref, inside=None):
    count = len(a_tiles)
    rows8 = HALF // 8
    lane = lax.broadcasted_iota(jnp.int32, (8, T), 1)
    sub = lax.broadcasted_iota(jnp.int32, (8, T), 0)

    def spread(x, s):
        return jnp.broadcast_to(x[s : s + 1, :], (8, T))

    for j0 in range(0, HALF, GROUP):
        if inside is not None and j0 == 6 * GROUP:
            inside()
        g = j0 // 8
        s0 = j0 - 8 * g
        state = []
        for m in range(count):
            cols = [
                [
                    jnp.broadcast_to(a_tiles[m][i][:, j0 + k : j0 + k + 1], (8, T))
                    for i in range(g, rows8)
                ]
                for k in range(GROUP)
            ]
            rows = [spread(a_tiles[m][g], s0 + k) for k in range(GROUP)]
            state.append((cols, rows))
        for k in range(GROUP):
            for m in range(count):
                cols, rows = state[m]
                rs = lax.rsqrt(spread(cols[k][0], s0 + k))
                cols[k] = [c * rs for c in cols[k]]
                rows[k] = rows[k] * rs
                for q in range(k + 1, GROUP):
                    f = spread(cols[k][0], s0 + q)
                    cols[q] = [c - l * f for c, l in zip(cols[q], cols[k])]
                    rows[q] = rows[q] - rows[k] * f
        for m in range(count):
            cols, rows = state[m]
            for k in range(GROUP):
                j = j0 + k
                r_ref[m, j : j + 1, :] = jnp.where(lane[:1] >= j, rows[k][:1], 0.0)
            last = s0 + GROUP == 8
            for i in range(g + 1 if last else g, rows8):
                a = a_tiles[m][i]
                for k in range(GROUP):
                    l = cols[k][i - g]
                    if i == g:
                        l = jnp.where(sub >= s0 + GROUP, l, 0.0)
                    a = a - l * rows[k]
                a_tiles[m][i] = a


def factor_block(a_list, u_ref, w_ref, r_ref, between, inside):
    lane = lax.broadcasted_iota(jnp.int32, (HALF, T), 1)
    row = lax.broadcasted_iota(jnp.int32, (HALF, T), 0)
    first = lane < HALF
    eye = jnp.where(lane == row + HALF, 1.0, 0.0).astype(jnp.float32)

    def turn(v):
        return pltpu.roll(v, HALF, 1)

    def tiles(v):
        return [v[8 * i : 8 * i + 8] for i in range(HALF // 8)]

    factor_tiles([tiles(jnp.where(first, a[:HALF], eye)) for a in a_list], r_ref)
    kept, second = [], []
    for m, a in enumerate(a_list):
        r1 = r_ref[m]
        w1 = turn(r1)
        top = dot(w1[:, :HALF], a[:HALF], ((1,), (0,)))
        rest = a[HALF:] - dot(top[:, HALF:], top, ((0,), (0,)))
        kept.append((jnp.where(first, w1, 0.0), top))
        second.append(tiles(jnp.where(first, turn(rest), eye)))
        u_ref[m, :HALF] = jnp.where(first, r1, top)
        w_ref[m, :HALF] = jnp.where(first, w1, 0.0)
    between()
    factor_tiles(second, r_ref, inside)
    for m, (w1, top) in enumerate(kept):
        r2 = r_ref[m]
        w2 = turn(r2)
        u_ref[m, HALF:] = jnp.where(first, 0.0, w2)
        low = dot(top[:, HALF:], w1, ((0,), (0,)))
        w_ref[m, HALF:] = jnp.where(first, -dot(w2[:, :HALF], low, ((1,), (0,))), r2)


CHUNKS = 4
NZ = 8
SIDE = 4
ROWS = 256
MESH = pl.DeviceIdType.MESH
FLOWS = [(0, 0), (1, 1), (0, 1), (1, 0)]


def first_hop(direction, t):
    return 1 if direction == t else 2


def ordered(tasks):
    rate = {"x": 43.0, "y": 43.0, "z": 43.0, "c": 300.0}
    link_free, arrival, done, order = {}, {}, set(), []
    now, left = 0.0, list(tasks)
    while left:
        best = None
        for n, task in enumerate(left):
            if all(a in done for a in task["after"]) and all(k in arrival for k in task["needs"]):
                start = max([now] + [arrival[k] for k in task["needs"]])
                if best is None or start < best[0]:
                    best = (start, n)
        start, n = best
        task = left.pop(n)
        now = start + task["time"]
        for key, link, kib in task["sends"]:
            begin = max(now, link_free.get(link, 0.0))
            link_free[link] = begin + kib / rate[link[0]]
            arrival[key] = link_free[link] + (1.0 if link[0] == "c" else 1.8)
        done.add(task["name"])
        order.append(task)
    return order


def bond_kernel(
    owner_ref, pairs_ref, sizes_ref, charges_ref, env_ref, block_ref, next_hbm, iso_ref, adv_ref,
    g0, g1, g2, g3, site_ref, env_v, part, send_b, recv_b, gp, gsend, grecv, gfull,
    bond_ref, root_ref, next_ref, s_ref, d_ref, u_ref, w_ref, r_ref,
    env_sem, next_sem, own_sem, ag_send, ag_recv, rs_send, rs_recv, gr_send, gr_recv, gg_send, gg_recv,
):
    gath = (g0, g1, g2, g3)
    sector, z = lax.axis_index("sector"), lax.axis_index("row")
    c = sector % 2
    x = (sector // 2) % SIDE
    y = sector // (2 * SIDE)

    def at(xx, yy, cc):
        return {"sector": ((yy % SIDE) * SIDE + xx % SIDE) * 2 + cc}

    def along(m, dmaj, dmin):
        return at(x + dmin, y + dmaj, c) if m == 0 else at(x + dmaj, y + dmin, c)

    major, minor = (y, x), (x, y)
    partner = at(x, y, 1 - c)
    up, down = {"row": (z + 1) % NZ}, {"row": (z + NZ - 1) % NZ}

    def slot(m, maj, mino):
        return 32 * m + ((maj % SIDE) * 2 + c) * SIDE + mino % SIDE

    barrier = pltpu.get_barrier_semaphore()
    partners = [along(0, 0, 1), along(0, 0, 3), along(0, 1, 0), along(0, 3, 0), partner, up, down]
    for device in partners:
        pl.semaphore_signal(barrier, inc=1, device_id=device, device_id_type=MESH)
    env_copy = pltpu.make_async_copy(env_ref, env_v, env_sem)
    env_copy.start()
    next_copy = pltpu.make_async_copy(next_hbm, next_ref, next_sem)
    next_copy.start()
    mine = [2 * sector, 2 * sector + 1]

    def find(n, found):
        return tuple(jnp.where(owner_ref[n] == slot_, n, f) for f, slot_ in zip(found, mine))

    sectors = lax.fori_loop(0, 64, find, (jnp.int32(0), jnp.int32(0)))
    limits, fields, source = [], [], []
    for t in range(2):
        limits.append(sizes_ref[sectors[t]] - z * ROWS)
        fields.append(charges_ref[sectors[t]].astype(jnp.float32) * (2.0 / 64))
        root_ref[t] = jnp.sqrt(jnp.full((8, T), sizes_ref[sectors[t]], jnp.int32).astype(jnp.float32))
        for n in range(4):
            place = owner_ref[pairs_ref[sectors[t], n]]
            px, py, pc = (place // 4) % SIDE, place // (4 * SIDE), (place // 2) % 2
            even = (py * 2 + pc) * SIDE + px
            odd = 32 + (px * 2 + pc) * SIDE + py
            source.append(jnp.where(place % 2 == 0, even, odd))
    row_ids = lax.broadcasted_iota(jnp.int32, (ROWS, T), 0)
    for j in range(CHUNKS):
        for m in range(2):
            value = block_ref[m, :, T * j : T * j + T].astype(jnp.float32)
            site_ref[j, m] = jnp.where(row_ids < limits[m], value, 0.0).astype(jnp.bfloat16)
    own = []
    for j in range(CHUNKS):
        for m in range(2):
            own.append(
                pltpu.make_async_copy(
                    site_ref.at[j, m], gath[j].at[slot(m, major[m], minor[m])], own_sem.at[j, m]
                )
            )
            own[-1].start()
    pl.semaphore_wait(barrier, len(partners))

    copies = {}

    def send(key, src, dst, ssem, rsem, device, late=False):
        copy = pltpu.make_async_remote_copy(
            src_ref=src, dst_ref=dst, send_sem=ssem, recv_sem=rsem, device_id=device, device_id_type=MESH
        )
        copies[key] = copy
        if not late:
            copy.start()

    def ag_send_one(j, m, n, ref, device, src=None):
        send((j, m, n), ref if src is None else src, ref, ag_send.at[j, m, n], ag_recv.at[j, m, n], device)

    def a1(j):
        for m in range(2):
            ref = gath[j].at[slot(m, major[m], minor[m])]
            ag_send_one(j, m, 0, ref, along(m, 0, 1), site_ref.at[j, m])
            ag_send_one(j, m, 1, ref, along(m, 0, 3), site_ref.at[j, m])

    def a2(j):
        for m in range(2):
            copies[j, m, 0].wait_recv()
            low = gath[j].at[slot(m, major[m], minor[m] + 3), pl.ds(0, ROWS // 2)]
            ag_send_one(j, m, 2, low, along(m, 0, 1))
            copies[j, m, 1].wait_recv()
            high = gath[j].at[slot(m, major[m], minor[m] + 1), pl.ds(ROWS // 2, ROWS // 2)]
            ag_send_one(j, m, 3, high, along(m, 0, 3))

    def group(j, m, dmaj, start=0, size=SIDE):
        return gath[j].at[pl.ds(slot(m, major[m] + dmaj, 0) + start, size)]

    def b1(j):
        for m in range(2):
            own[2 * j + m].wait()
            copies[j, m, 2].wait_recv()
            copies[j, m, 3].wait_recv()
            ag_send_one(j, m, 4, group(j, m, 0, 0, 2), along(m, 1, 0))
            ag_send_one(j, m, 5, group(j, m, 0, 2, 2), along(m, 3, 0))
            ag_send_one(j, m, 12, group(j, m, 0, 2, 2), along(m, 1, 0))
            ag_send_one(j, m, 13, group(j, m, 0, 0, 2), along(m, 3, 0))
            ag_send_one(j, m, 8, group(j, m, 0), partner)

    def b2(j):
        for m in range(2):
            copies[j, m, 4].wait_recv()
            ag_send_one(j, m, 6, group(j, m, 3, 0, 2), along(m, 1, 0))
            copies[j, m, 5].wait_recv()
            ag_send_one(j, m, 7, group(j, m, 1, 2, 2), along(m, 3, 0))

    def b2c(j):
        for m in range(2):
            copies[j, m, 12].wait_recv()
            copies[j, m, 13].wait_recv()
            ag_send_one(j, m, 9, group(j, m, 3), partner)
            ag_send_one(j, m, 10, group(j, m, 1), partner)

    def b3(j):
        for m in range(2):
            copies[j, m, 6].wait_recv()
            copies[j, m, 7].wait_recv()
            ag_send_one(j, m, 11, group(j, m, 2), partner)

    def ready(j):
        for m in range(2):
            for n in (8, 9, 10, 11):
                copies[j, m, n].wait_recv()
        if j == 0:
            env_copy.wait()

    def multiply(j, r):
        def one(n, carry):
            t = n % 2
            o = (n // 2) * (NZ - 2 * r) + r
            first = pl.multiple_of(((z + o) % NZ) * ROWS, ROWS)
            total = None
            for k in range(4):
                term = jnp.dot(
                    env_v[t, k, pl.ds(first, ROWS), :],
                    gath[j][jnp.where(t == 0, source[k], source[4 + k])],
                    preferred_element_type=jnp.float32,
                )
                total = term if total is None else total + term
            part[j, o, t] = total
            return carry

        lax.fori_loop(0, 2 if r in (0, 4) else 4, one, 0)

    def hop(j, s, direction, t):
        o = 5 - s if direction == 0 else 3 + s
        value = part[j, o, t]
        if s > first_hop(direction, t):
            copies["r", j, s - 1, direction, t].wait_recv()
            value = value + recv_b[j, direction, t, s - 2].astype(jnp.float32)
        send_b[j, direction, t, s - 1] = value.astype(jnp.bfloat16)
        send(
            ("r", j, s, direction, t),
            send_b.at[j, direction, t, s - 1],
            recv_b.at[j, direction, t, s - 1],
            rs_send.at[j, direction, t, s - 1],
            rs_recv.at[j, direction, t, s - 1],
            up if direction == 0 else down,
        )

    def finish(j, t):
        copies["r", j, 4, 0, t].wait_recv()
        copies["r", j, 4, 1, t].wait_recv()
        cols = pl.ds(T * j, T)
        total = part[j, 0, t] + fields[t] * site_ref[j, t].astype(jnp.float32)
        total = total + recv_b[j, 0, t, 3].astype(jnp.float32) + recv_b[j, 1, t, 3].astype(jnp.float32)
        bond_ref[t, :, cols] = jnp.where(row_ids < limits[t], total, 0.0)

    def grams(j):
        for t in range(2):
            for i in range(j + 1):
                value = dot(bond_ref[t, :, T * i : T * i + T], bond_ref[t, :, T * j : T * j + T], ((0,), (0,)))
                for q in range(NZ):
                    gp[j, q, t, i] = value[16 * q : 16 * q + 16]

    for j in range(CHUNKS):
        for s in range(1, 5):
            for direction, t in FLOWS:
                device = up if direction == 0 else down
                if s >= first_hop(direction, t):
                    send(
                        ("g", j, s, direction, t),
                        gsend.at[j, direction, t, s - 1, pl.ds(0, j + 1)],
                        grecv.at[j, direction, t, s - 1, pl.ds(0, j + 1)],
                        gr_send.at[j, direction, t, s - 1],
                        gr_recv.at[j, direction, t, s - 1],
                        device, late=True,
                    )
                if s < 4 or direction == t:
                    q = (z + NZ - (s - 1)) % NZ if direction == 0 else (z + s - 1) % NZ
                    piece = gfull.at[q, t, pl.ds(j * (j + 1) // 2, j + 1)]
                    send(
                        ("f", j, s, direction, t), piece, piece,
                        gg_send.at[j, direction, t, s - 1], gg_recv.at[j, direction, t, s - 1],
                        device, late=True,
                    )

    def gram_hop(j, s, direction, t):
        o = 5 - s if direction == 0 else 3 + s
        value = gp[j, (z + o) % NZ, t, : j + 1]
        if s > first_hop(direction, t):
            copies["g", j, s - 1, direction, t].wait_recv()
            value = value + grecv[j, direction, t, s - 2, : j + 1]
        gsend[j, direction, t, s - 1, : j + 1] = value
        copies["g", j, s, direction, t].start()

    def gram_sum(j, t):
        copies["g", j, 4, 0, t].wait_recv()
        copies["g", j, 4, 1, t].wait_recv()
        total = gp[j, z, t, : j + 1] + grecv[j, 0, t, 3, : j + 1] + grecv[j, 1, t, 3, : j + 1]
        gfull[z, t, j * (j + 1) // 2 : (j + 1) * (j + 2) // 2] = total

    def gram_round(j, s, direction, t):
        if s > 1:
            copies["f", j, s - 1, direction, t].wait_recv()
        copies["f", j, s, direction, t].start()

    def hops(j, s):
        for direction, t in FLOWS:
            if s >= first_hop(direction, t):
                gram_hop(j, s, direction, t)

    def sums(j):
        for t in range(2):
            gram_sum(j, t)

    def rounds(j, s):
        for direction, t in FLOWS:
            if s < 4 or direction == t:
                gram_round(j, s, direction, t)

    def last(j):
        for direction, t in FLOWS:
            copies["f", j, 4 if direction == t else 3, direction, t].wait_recv()
        for i in range(j + 1):
            for m in range(2):
                for q in range(NZ):
                    s_ref[m, i, j, 16 * q : 16 * q + 16, :] = gfull[q, m, j * (j + 1) // 2 + i]

    late_steps = {
        (0, 0): lambda: (last(0), hops(3, 1), sums(2), rounds(2, 1)),
        (0, 2): lambda: (hops(3, 2), rounds(2, 2)),
        (0, 3): lambda: (hops(3, 3), rounds(2, 3)),
        (1, 0): lambda: last(1),
        (1, 1): lambda: (hops(3, 4), rounds(2, 4)),
        (1, 2): lambda: (sums(3), rounds(3, 1)),
        (1, 3): lambda: rounds(3, 2),
        (2, 0): lambda: last(2),
        (2, 1): lambda: rounds(3, 3),
        (2, 2): lambda: rounds(3, 4),
        (3, 0): lambda: last(3),
    }

    def point(p, n):
        for (block, place), run in late_steps.items():
            if place == n:

                @pl.when(p == block)
                def _(run=run):
                    run()

    tasks = []

    def task(name, emit, time, needs=(), after=(), sends=()):
        tasks.append(dict(name=name, emit=emit, time=time, needs=needs, after=after, sends=sends))

    def axes(m):
        return ("x", "y") if m == 0 else ("y", "x")

    for j in range(CHUNKS):
        ms = range(2)
        mins, majs = [axes(m)[0] for m in ms], [axes(m)[1] for m in ms]
        task(("a1", j), lambda j=j: a1(j), 0.1,
             after=[[], [("a1", 0)], [("a2", 0)], [("b1", 1)]][j],
             sends=[((j, m, n), mins[m] + str(n), 64) for m in ms for n in (0, 1)])
        task(("a2", j), lambda j=j: a2(j), 0.1, needs=[(j, m, n) for m in ms for n in (0, 1)],
             sends=[((j, m, n + 2), mins[m] + str(n), 32) for m in ms for n in (0, 1)])
        task(("b1", j), lambda j=j: b1(j), 0.1, needs=[(j, m, n) for m in ms for n in (2, 3)],
             after=[("b2", j - 1)] if j else [],
             sends=[((j, m, n + 4 + late), majs[m] + str(n), 128) for m in ms for late in (0, 8) for n in (0, 1)]
             + [((j, m, 8), "c", 256) for m in ms])
        task(("b2", j), lambda j=j: b2(j), 0.1, needs=[(j, m, n) for m in ms for n in (4, 5)],
             sends=[((j, m, n + 6), majs[m] + str(n), 128) for m in ms for n in (0, 1)])
        task(("b2c", j), lambda j=j: b2c(j), 0.1, needs=[(j, m, n) for m in ms for n in (12, 13)],
             after=[("b2", j)], sends=[((j, m, n), "c", 256) for m in ms for n in (9, 10)])
        task(("b3", j), lambda j=j: b3(j), 0.1, needs=[(j, m, n) for m in ms for n in (6, 7)], after=[("b2c", j)],
             sends=[((j, m, 11), "c", 256) for m in ms])
        task(("ready", j), lambda j=j: ready(j), 0.1, needs=[(j, m, n) for m in ms for n in (8, 9, 10, 11)])
        before = ("ready", j)
        for r in (4, 3, 2, 1, 0):
            task(("mm", j, r), lambda j=j, r=r: multiply(j, r), 0.4 if r in (0, 4) else 0.8, after=[before])
            before = ("mm", j, r)
            if r == 0:
                continue
            s = 5 - r
            for direction, t in FLOWS:
                if s >= first_hop(direction, t):
                    more = s > first_hop(direction, t)
                    task(("hop", j, s, direction, t),
                         lambda j=j, s=s, direction=direction, t=t: hop(j, s, direction, t), 0.1,
                         needs=[("r", j, s - 1, direction, t)] if more else [], after=[before],
                         sends=[(("r", j, s, direction, t), "z" + str(direction), 64)])
        for t in range(2):
            task(("finish", j, t), lambda j=j, t=t: finish(j, t), 0.1,
                 needs=[("r", j, 4, 0, t), ("r", j, 4, 1, t)], after=[("mm", j, 0)])
        task(("gram", j), lambda j=j: grams(j), 0.4 + 0.4 * j,
             after=[("finish", j, 0), ("finish", j, 1)] + ([("gram", j - 1)] if j else []))
        for s in range(1, 5):
            for direction, t in FLOWS:
                if s >= first_hop(direction, t) and j < 3:
                    more = s > first_hop(direction, t)
                    task(("ghop", j, s, direction, t),
                         lambda j=j, s=s, direction=direction, t=t: gram_hop(j, s, direction, t), 0.1,
                         needs=[("g", j, s - 1, direction, t)] if more else [], after=[("gram", j)],
                         sends=[(("g", j, s, direction, t), "z" + str(direction), 8 * (j + 1))])
        for t in range(2 if j < 2 else 0):
            task(("gsum", j, t), lambda j=j, t=t: gram_sum(j, t), 0.1,
                 needs=[("g", j, 4, 0, t), ("g", j, 4, 1, t)], after=[("gram", j)])
        for s in range(1, 5):
            for direction, t in FLOWS:
                if j < 2 and (s < 4 or direction == t):
                    task(("ground", j, s, direction, t),
                         lambda j=j, s=s, direction=direction, t=t: gram_round(j, s, direction, t), 0.1,
                         needs=[("f", j, s - 1, direction, t)] if s > 1 else [], after=[("gsum", j, t)],
                         sends=[(("f", j, s, direction, t), "z" + str(direction), 8 * (j + 1))])
    for item in ordered(tasks):
        item["emit"]()

    def block(p, carry):
        point(p, 0)
        def column(i, c):
            def above(k, c2):
                for m in range(2):
                    s_ref[m, i, p] = s_ref[m, i, p] - dot(s_ref[m, k, i], s_ref[m, k, p], ((0,), (0,)))
                return c2

            lax.fori_loop(0, i, above, 0)
            for m in range(2):
                value = dot(d_ref[m, i], s_ref[m, i, p], ((1,), (0,)))
                s_ref[m, i, p] = value
                s_ref[m, p, p] = s_ref[m, p, p] - dot(value, value, ((0,), (0,)))
            return c

        lax.fori_loop(0, p, column, 0)
        point(p, 1)
        factor_block(
            [s_ref[m, p, p] for m in range(2)], u_ref, w_ref, r_ref,
            lambda: point(p, 2), lambda: point(p, 3),
        )
        for m in range(2):
            d_ref[m, p] = w_ref[m]
            s_ref[m, p, p] = u_ref[m]
        cols = pl.ds(pl.multiple_of(p * T, T), T)

        def left(i, c):
            before = pl.ds(pl.multiple_of(i * T, T), T)
            for m in range(2):
                term = dot(bond_ref[m, :, before], s_ref[m, i, p], ((1,), (0,)))
                bond_ref[m, :, cols] = bond_ref[m, :, cols] - term
            return c

        lax.fori_loop(0, p, left, 0)
        for m in range(2):
            value = dot(bond_ref[m, :, cols], d_ref[m, p], ((1,), (1,)))
            bond_ref[m, :, cols] = value
            iso_ref[m, :, cols] = value * root_ref[m, :1, :]
        return carry

    lax.fori_loop(0, NB, block, 0)
    next_copy.wait()
    row16 = lax.broadcasted_iota(jnp.int32, (16, T), 0)
    lane16 = lax.broadcasted_iota(jnp.int32, (16, T), 1)
    for m in range(2):
        trace = jnp.zeros((16, T), jnp.float32)
        for p in range(NB):
            for q in range(NZ):
                trace = trace + jnp.where(lane16 == row16 + 16 * q, gfull[q, m, p * (p + 3) // 2], 0.0)
        scale = lax.rsqrt(jnp.full((1, T), jnp.sum(trace) / (NB * T) + 1e-6, jnp.float32))
        for p in range(NB):
            total = None
            for i in range(p, NB):
                up_block = (s_ref[m, p, i] * scale).astype(jnp.bfloat16)
                term = dot(up_block, next_ref[m, T * i : T * i + T, :], ((1,), (0,)), None)
                total = term if total is None else total + term
            adv_ref[m, T * p : T * p + T, :] = total.astype(jnp.bfloat16)
    for copy in copies.values():
        copy.wait_send()


def site_step(owner, pairs, sizes, charges, environment, site_block, next_site):
    vmem, anywhere = pl.BlockSpec(memory_space=pltpu.VMEM), pl.BlockSpec(memory_space=pl.ANY)
    bf, f32 = jnp.bfloat16, jnp.float32
    dma = pltpu.SemaphoreType.DMA
    blocks = NB * (NB + 1) // 2
    return pl.pallas_call(
        bond_kernel,
        out_shape=(
            jax.ShapeDtypeStruct(site_block.shape, f32),
            jax.ShapeDtypeStruct(next_site.shape, bf),
        ),
        in_specs=[pl.BlockSpec(memory_space=pltpu.SMEM)] * 4 + [anywhere, vmem, anywhere],
        out_specs=(vmem, vmem),
        scratch_shapes=[pltpu.VMEM((64, ROWS, T), bf)] * CHUNKS
        + [
            pltpu.VMEM((CHUNKS, 2, ROWS, T), bf),
            pltpu.VMEM(environment.shape, bf),
            pltpu.VMEM((CHUNKS, NZ, 2, ROWS, T), f32),
            pltpu.VMEM((CHUNKS, 2, 2, 4, ROWS, T), bf),
            pltpu.VMEM((CHUNKS, 2, 2, 4, ROWS, T), bf),
            pltpu.VMEM((CHUNKS, NZ, 2, NB, 16, T), f32),
            pltpu.VMEM((CHUNKS, 2, 2, 4, NB, 16, T), f32),
            pltpu.VMEM((CHUNKS, 2, 2, 4, NB, 16, T), f32),
            pltpu.VMEM((NZ, 2, blocks, 16, T), f32),
            pltpu.VMEM(site_block.shape, f32),
            pltpu.VMEM((2, 8, T), f32),
            pltpu.VMEM(next_site.shape, bf),
            pltpu.VMEM((2, NB, NB, T, T), f32),
            pltpu.VMEM((2, NB, T, T), f32),
            pltpu.VMEM((2, T, T), f32),
            pltpu.VMEM((2, T, T), f32),
            pltpu.VMEM((2, HALF, T), f32),
            dma,
            dma,
            dma((CHUNKS, 2)),
            dma((CHUNKS, 2, 14)),
            dma((CHUNKS, 2, 14)),
            dma((CHUNKS, 2, 2, 4)),
            dma((CHUNKS, 2, 2, 4)),
            dma((CHUNKS, 2, 2, 4)),
            dma((CHUNKS, 2, 2, 4)),
            dma((CHUNKS, 2, 2, 4)),
            dma((CHUNKS, 2, 2, 4)),
        ],
        compiler_params=pltpu.CompilerParams(
            vmem_limit_bytes=63 * 1024 * 1024, collective_id=0, has_side_effects=True
        ),
        name="bond",
    )(owner, pairs, sizes, charges, environment, site_block, next_site)


def local(environment, site_block, next_site, charges, sizes, pairs, owner):
    iso, advanced = site_step(
        owner, pairs, sizes, charges, environment, site_block, next_site
    )
    return (jnp.swapaxes(iso, 0, 1), advanced)


def solution(mesh):
    return jax.shard_map(
        local,
        mesh=mesh,
        in_specs=(
            P("sector", None, None, "row"),
            P("sector", "row", None),
            P("sector", None, "row"),
            P(),
            P(),
            P(),
            P(),
        ),
        out_specs=(P("row", "sector", None), P("sector", None, "row")),
        check_vma=False,
    )
```
